256 devices in a mesh: cfg: 2 (over core), req: 128 (over y, z, x).
Axes of the slice: x: 4, y: 4, z: 8, core: 2. Of those that a mesh axis runs over, the one named last changes fastest.
Arguments:
- query_rows: bfloat16 [2, 65536, 2560], P('cfg', 'req'), may hold values from -32 to 32
- key_rows: bfloat16 [2, 65536, 2560], P('cfg', 'req'), may hold values from -6 to 6
- value_rows: bfloat16 [2, 65536, 2560], P('cfg', 'req'), may hold values from -600 to 600
- positions: int32 [3, 65536], P(None, 'req'), may hold values from 0 to 51
- latents: float32 [65536, 64], P('req', 'cfg'), may hold values from -6 to 6
- w_head: bfloat16 [2560, 64], replicated, may hold values from -0.125 to 0.125
- modulation: float32 [2, 2560], replicated, may hold values from -0.5 to 1
- guide_scale: float32 [1], replicated, may hold values from 4 to 6
- step_sizes: float32 [256], replicated, may hold values from -0.4 to -0.1
- lengths: int32 [256], replicated, may hold values from 1 to 512, 65536 in all
Outputs:
- next_latents: float32 [65536, 64], P('req', 'cfg')
The draws below stay inside these ranges and needn't reach their ends.
Inputs may be any that keep to these rules, and one draw needn't show every extreme that they name: Videos are laid end to end in the given order and their lengths sum to 65536.
All inputs are finite; a program needn't handle non-finite values.
Results may differ from the reference program's by a relative error of at most 0.0059.
Values may be sent and summed in bfloat16 or wider, within the bound.
A program may use at most 128 MiB of HBM per device.

```python
import math
import jax
import jax.numpy as jnp
import numpy as np
from jax import lax

HD = 128
LATC = 64
LMAX = 512
ROWS = 512
HWD = 2560
TOKENS = 65536
NV = 256


def query_key_pair(key):
    full_shape = (2, TOKENS, HWD)
    query_seed = jax.random.fold_in(key, 101)
    key_seed = jax.random.fold_in(key, 102)
    query_draw = jnp.clip(jax.random.normal(query_seed, full_shape, jnp.float32), -6.0, 6.0)
    key_draw = jnp.clip(jax.random.normal(key_seed, full_shape, jnp.float32), -6.0, 6.0)
    return (query_draw, key_draw)


def draw_query_rows(key, part):
    return query_key_pair(key)[0].astype(jnp.bfloat16)


def draw_key_rows(key, part):
    return query_key_pair(key)[1].astype(jnp.bfloat16)


def draw_value_rows(key, part):
    base_seed = jax.random.fold_in(key, 201)
    row_seed = jax.random.fold_in(key, 202)
    column_seed = jax.random.fold_in(key, 203)
    base = jnp.clip(jax.random.normal(base_seed, (2, TOKENS, HWD), jnp.float32), -6.0, 6.0)
    row_scale = jnp.exp(jax.random.uniform(row_seed, (2, TOKENS, 1), jnp.float32, 0.0, math.log(10.0)))
    column_scale = jnp.exp(jax.random.uniform(column_seed, (1, 1, HWD), jnp.float32, 0.0, math.log(10.0)))
    return (base * row_scale * column_scale).astype(jnp.bfloat16)


def plant(entries, rng, smallest, largest):
    spot = [jax.random.randint(jax.random.fold_in(rng, axis), (), 0, length) for axis, length in enumerate(entries.shape)]
    widest = entries.shape.index(max(entries.shape))
    beside = spot[:widest] + [(spot[widest] + 1) % entries.shape[widest]] + spot[widest + 1:]
    return entries.at[tuple(spot)].set(smallest).at[tuple(beside)].set(largest)


def levels(own_key, shape, cuts, smallest, largest):
    level, own = 1.0, jax.random.fold_in(own_key, 6)
    for axis_at, blocks in cuts:
        draws = jnp.exp(jax.random.uniform(jax.random.fold_in(own, axis_at), (blocks,), jnp.float32, smallest / len(cuts), largest / len(cuts)))
        level = level * jnp.repeat(draws, shape[axis_at] // blocks).reshape([-1 if axis == axis_at else 1 for axis in range(len(shape))])
    return level


def length_profile(number_of, total, reach, skew):
    weights = [(1 << 20) // math.isqrt(rank ** skew) + 1 for rank in range(2, number_of + 1)]
    spare, given = total - reach - (number_of - 1), [1] * (number_of - 1)
    while spare > 0:
        candidates = [i for i in range(number_of - 1) if given[i] < reach]
        mass, left = sum([weights[i] for i in candidates]), spare
        for i in candidates:
            extra = min(reach - given[i], max(1, left * weights[i] // mass), spare)
            given[i] = given[i] + extra
            spare = spare - extra
    return np.array([reach] + given)


def ragged_sizes(own_key, count, total, most, skew):
    if count == 2:
        one = jax.random.randint(own_key, (), max(1, total - most), min(most, total - 1) + 1)
        return jnp.stack([one, total - one])
    sizes = jnp.asarray(length_profile(count, total, most, skew), jnp.int32)
    couples = (count - 1) // 2
    donor, receiver = sizes[1:1 + 2 * couples:2], sizes[2:2 + 2 * couples:2]
    margin = jnp.minimum(donor - 1, most - receiver)
    moved = jax.random.randint(jax.random.fold_in(own_key, 1), (couples,), 0, 1 << 20) % (margin + 1)
    sizes = sizes.at[1:1 + 2 * couples:2].set(donor - moved).at[2:2 + 2 * couples:2].set(receiver + moved)
    return sizes[jax.random.permutation(jax.random.fold_in(own_key, 2), count)]


def scatter_about(key, dims, scale, most, pieces=(), kind=jnp.bfloat16):
    array = jax.random.normal(key, dims, jnp.float32) * scale
    if len(pieces) > 0:
        array = levels(key, dims, pieces, -0.22, 0.18) * array
    return jnp.clip(array, min=-most, max=most).astype(kind)


def setup_inputs(seed: int = 0) -> dict:
    splits = jax.random.split(jax.random.key(seed), 11)
    query_rows = draw_query_rows(jax.random.fold_in(splits[10], 71), 0)
    key_rows = draw_key_rows(jax.random.fold_in(splits[10], 71), 0)
    value_rows = draw_value_rows(jax.random.fold_in(splits[10], 71), 0)
    positions = plant(jax.random.randint(splits[3], (3, TOKENS), 0, 52), jax.random.fold_in(splits[3], 1), 0, 51).astype(jnp.int32)
    latents = scatter_about(splits[4], (TOKENS, LATC), 1.0, 6.0, ((0, 128), (1, 2)), jnp.float32)
    w_head = scatter_about(splits[5], (HWD, LATC), HWD ** -0.5, 0.125)
    modulation = jnp.clip(jax.random.uniform(splits[6], (2, HWD), jnp.float32, -0.5, 1.0), -0.5, 1.0)
    guide_scale = jnp.clip(jax.random.uniform(splits[7], (1,), jnp.float32, 4.0, 6.0), 4.0, 6.0)
    step_sizes = jnp.clip(jax.random.uniform(splits[8], (NV,), jnp.float32, -0.4, -0.1), -0.4, -0.1)
    lengths = ragged_sizes(splits[9], NV, TOKENS, LMAX, 1).astype(jnp.int32)
    return dict(query_rows=query_rows, key_rows=key_rows, value_rows=value_rows, positions=positions, latents=latents, w_head=w_head, modulation=modulation, guide_scale=guide_scale, step_sizes=step_sizes, lengths=lengths)


masked_score = -1e+30
rope_theta = 10000.0

def angles(positions):
    pair_total = HD // 2
    side_pairs = HD // 6
    time_pairs = pair_total - 2 * side_pairs
    column = jnp.arange(pair_total, dtype=jnp.int32)
    in_time = column < time_pairs
    in_height = (column >= time_pairs) & (column < time_pairs + side_pairs)
    in_width = column >= time_pairs + side_pairs
    local_index = jnp.where(in_time, column, jnp.where(in_height, column - time_pairs, column - time_pairs - side_pairs))
    axis_pairs = jnp.where(in_time, time_pairs, side_pairs)
    frequency = jnp.exp(-(local_index.astype(jnp.float32) / axis_pairs.astype(jnp.float32)) * math.log(rope_theta))
    selector = jnp.stack([in_time, in_height, in_width]).astype(jnp.float32) * frequency[None, :]
    placed = positions.astype(jnp.float32)
    return placed[0][:, None] * selector[0][None, :] + placed[1][:, None] * selector[1][None, :] + placed[2][:, None] * selector[2][None, :]

def rotate(features, angle_table):
    row_total = features.shape[0]
    heads_here = features.shape[1] // HD
    paired = features.astype(jnp.float32).reshape(row_total, heads_here, HD // 2, 2)
    cosine = jnp.cos(angle_table)[:, None, :]
    sine_part = jnp.sin(angle_table)[:, None, :]
    real_part = paired[..., 0]
    imag_part = paired[..., 1]
    turned = jnp.stack([real_part * cosine - imag_part * sine_part, real_part * sine_part + imag_part * cosine], axis=-1)
    return turned.reshape(row_total, heads_here * HD).astype(jnp.bfloat16)

def video_of(global_rows, video_ends, row_count):
    inside = (global_rows >= 0) & (global_rows < row_count)
    counted = lax.optimization_barrier(jnp.sum((video_ends[None, :] <= global_rows[:, None]).astype(jnp.int32), axis=1))
    return jnp.where(inside, counted, -1).astype(jnp.int32)

def attend(query_block, window, first_row, video_ends, row_count):
    rows_here = query_block.shape[0]
    feature_count = query_block.shape[1]
    heads_here = feature_count // HD
    key_count = window.shape[0]
    query_video = video_of(first_row + jnp.arange(rows_here, dtype=jnp.int32), video_ends, row_count)
    key_first = first_row - (key_count - rows_here) // 2
    key_video = video_of(key_first + jnp.arange(key_count, dtype=jnp.int32), video_ends, row_count)
    same_video = query_video[:, None] == key_video[None, :]
    score_scale = 1.0 / math.sqrt(HD)
    query_heads = query_block.reshape(rows_here, heads_here, HD).transpose(1, 0, 2)
    key_heads = window[:, :feature_count].reshape(key_count, heads_here, HD).transpose(1, 0, 2)
    value_heads = window[:, feature_count:].reshape(key_count, heads_here, HD).transpose(1, 0, 2)

    def one_head(operands):
        query_head, key_head, value_head = operands
        scores = jnp.dot(query_head, key_head.T, preferred_element_type=jnp.float32) * score_scale
        scores = jnp.where(same_video, scores, masked_score)
        row_max = lax.optimization_barrier(jnp.max(scores, axis=1, keepdims=True))
        weights = jnp.exp(scores - row_max)
        denominator = lax.optimization_barrier(jnp.sum(weights, axis=1, keepdims=True))
        summed = jnp.dot(weights.astype(jnp.bfloat16), value_head, preferred_element_type=jnp.float32)
        return (summed / denominator).astype(jnp.bfloat16)
    outputs = lax.map(one_head, (query_heads, key_heads, value_heads))
    return outputs.transpose(1, 0, 2).reshape(rows_here, feature_count)

def project(attended, modulation, w_head):
    widened = attended.astype(jnp.float32)
    mean_square = lax.optimization_barrier(jnp.mean(widened * widened, axis=1, keepdims=True))
    normed = widened * lax.rsqrt(mean_square + 1e-06) * (1.0 + modulation[1][None, :]) + modulation[0][None, :]
    return jnp.dot(normed.astype(jnp.bfloat16), w_head, preferred_element_type=jnp.float32)

def step_rows(video_ids, step_sizes):
    video_count = step_sizes.shape[0]
    chosen = video_ids[:, None] == jnp.arange(video_count, dtype=jnp.int32)[None, :]
    return lax.optimization_barrier(jnp.sum(jnp.where(chosen, step_sizes[None, :], jnp.zeros_like(step_sizes)[None, :]), axis=1))

def reference(query_rows, key_rows, value_rows, positions, latents, w_head, modulation, guide_scale, step_sizes, lengths):
    row_count = TOKENS
    angle_table = angles(positions)
    video_ends = jnp.cumsum(lengths).astype(jnp.int32)
    margin_count = ROWS
    window_count = 3 * ROWS
    velocities = []
    for parity in range(2):
        query_rot = rotate(query_rows[parity], angle_table)
        key_rot = rotate(key_rows[parity], angle_table)
        joined = jnp.concatenate([key_rot, value_rows[parity]], axis=1)
        padded = jnp.pad(joined, ((margin_count, margin_count), (0, 0)))

        def one_block(block_index, query_rot=query_rot, padded=padded):
            first_row = (block_index * ROWS).astype(jnp.int32)
            query_block = lax.dynamic_slice_in_dim(query_rot, first_row, ROWS, 0)
            window = lax.dynamic_slice_in_dim(padded, first_row, window_count, 0)
            return attend(query_block, window, first_row, video_ends, row_count)
        attended = lax.map(one_block, jnp.arange(TOKENS // ROWS, dtype=jnp.int32)).reshape(TOKENS, HWD)
        velocities.append(project(attended, modulation, w_head))
    guided = velocities[1] + guide_scale[0] * (velocities[0] - velocities[1])
    video_ids = video_of(jnp.arange(TOKENS, dtype=jnp.int32), video_ends, row_count)
    return latents + step_rows(video_ids, step_sizes)[:, None] * guided
```

```python
import functools
import math

import jax
import jax.numpy as jnp
import numpy as np
from jax import lax
from jax.experimental import pallas as pl
from jax.experimental.pallas import tpu as pltpu
from jax.sharding import PartitionSpec as P


HD = 128
ROWS = 512
LATC = 64
TILE = 16
TILES = ROWS // TILE
FAR = 24
REACH = FAR * TILE
SPAN = 2 * ROWS + 128
ACCR = 72
masked_score = -1e30
rope_theta = 10000.0
MESH = pl.DeviceIdType.MESH
SMEM = pl.BlockSpec(memory_space=pltpu.SMEM)
VMEM = pl.BlockSpec(memory_space=pltpu.VMEM)
ANY = pl.BlockSpec(memory_space=pl.ANY)


def share_static(ta, tb, heads):
    if ta > FAR:
        return 0
    if tb > FAR:
        return heads
    costs = [max(n * ta, (heads - n) * tb) for n in range(heads + 1)]
    return costs.index(min(costs))


def capacity(heads):
    most = 0
    for ta in range(1, TILES + 1):
        for tb in range(1, TILES + 2 - ta):
            n = share_static(ta, tb, heads)
            most = max(most, n * ta, (heads - n) * tb)
    return most


def chunk_tiles(heads):
    cap = capacity(heads)
    if cap >= 150:
        return (48, 48, 42, cap - 138)
    return (FAR, cap - FAR)


def share(ta, tb, heads):
    best = heads * tb
    chosen = jnp.int32(0)
    for n in range(1, heads + 1):
        cost = jnp.maximum(n * ta, (heads - n) * tb)
        better = cost < best
        best = jnp.where(better, cost, best)
        chosen = jnp.where(better, n, chosen)
    chosen = jnp.where(tb > FAR, heads, chosen)
    return jnp.where(ta > FAR, 0, chosen)


def selector():
    pair_total = HD // 2
    side = HD // 6
    time = pair_total - 2 * side
    axis = np.array([0] * time + [1] * side + [2] * side)
    local = np.array(list(range(time)) + list(range(side)) * 2, np.float32)
    pairs = np.array([time] * time + [side] * (2 * side), np.float32)
    frequency = np.exp(-(local / pairs) * np.float32(math.log(rope_theta))).astype(np.float32)
    table = np.zeros((4, TILE, HD), np.float32)
    for group in range(4):
        for lane in range(HD):
            table[group, axis[lane // 2] * 4 + group, lane] = frequency[lane // 2]
    parts = []
    rest = table
    for _ in range(3):
        part = rest.astype(jnp.bfloat16)
        parts.append(part)
        rest = rest - part.astype(np.float32)
    return np.stack(parts)


def turner():
    table = np.zeros((HD, HD), np.float32)
    for pair in range(HD // 2):
        table[2 * pair + 1, 2 * pair] = -1.0
        table[2 * pair, 2 * pair + 1] = 1.0
    return table.astype(jnp.bfloat16)


def cdiv(value, unit):
    return (value + unit - 1) // unit


def pack_kernel(heads, chunks, lens_ref, pos_ref, q_ref, k_ref, v_ref, scal_ref, place_ref, *rest):
    count = len(chunks)
    right_refs, left_refs = rest[:count], rest[count : 2 * count]
    rows_in, packed, in_sem, out_sem = rest[2 * count :]
    groups = 4 if heads % 4 == 0 else 1
    width = heads // groups * HD
    loads = []
    for group in range(groups):
        columns = pl.ds(group * width, width)
        for j, source in enumerate((q_ref, k_ref, v_ref)):
            copy = pltpu.make_async_copy(
                source.at[:, :, columns],
                rows_in.at[j, pl.ds(0, TILES), :, columns],
                in_sem.at[group, j],
            )
            copy.start()
            loads.append(copy)
    low = lax.axis_index("req") * ROWS
    high = low + ROWS

    def scan(i, carry):
        end, start_low, end_low, start_high, end_high = carry
        start = end
        end = start + lens_ref[i]
        before_low = start < low
        before_high = start < high
        return (
            end,
            jnp.where(before_low, start, start_low),
            jnp.where(before_low, end, end_low),
            jnp.where(before_high, start, start_high),
            jnp.where(before_high, end, end_high),
        )

    zero = jnp.int32(0)
    _, start_low, end_low, start_high, end_high = lax.fori_loop(
        0, lens_ref.shape[0], scan, (zero, low, low, high, high), unroll=8
    )
    cut_low = end_low > low
    cut_high = end_high > high
    a_low = jnp.where(cut_low, low - start_low, 0)
    b_low = jnp.where(cut_low, end_low - low, 0)
    a_high = jnp.where(cut_high, high - start_high, 0)
    b_high = jnp.where(cut_high, end_high - high, 0)
    n_low = share(cdiv(a_low, TILE), cdiv(b_low, TILE), heads)
    n_high = share(cdiv(a_high, TILE), cdiv(b_high, TILE), heads)
    for i, value in enumerate((a_low, b_low, n_low, a_high, b_high, n_high)):
        scal_ref[i] = value
    scal_ref[6] = zero
    scal_ref[7] = zero

    placed = pos_ref[...].astype(jnp.float32)
    pieces = [placed[a : a + 1, g * HD : (g + 1) * HD] for a in range(3) for g in range(4)]
    pieces.append(jnp.zeros((TILE - 12, HD), jnp.float32))
    place_ref[...] = jnp.concatenate(pieces, axis=0).astype(jnp.bfloat16)
    for copy in loads:
        copy.wait()

    def pack(direction, first_tile, first_head, tiles, total):
        def one(slot, carry):
            columns = pl.ds(pl.multiple_of((first_head + slot) * HD, HD), HD)
            for j in range(3):
                packed[direction, j, pl.ds(slot * tiles, FAR)] = rows_in[
                    j, pl.ds(first_tile, FAR), :, columns
                ]
            return carry

        lax.fori_loop(0, total, one, 0)

    ta, tb = cdiv(a_high, TILE), cdiv(b_low, TILE)
    pack(0, TILES - ta, 0, ta, jnp.where(a_high > 0, n_high, 0))
    pack(1, 0, n_low, tb, jnp.where(b_low > 0, heads - n_low, 0))
    stores = []
    for direction, targets in enumerate((right_refs, left_refs)):
        begin = 0
        for c, tiles in enumerate(chunks):
            copy = pltpu.make_async_copy(
                packed.at[direction, :, pl.ds(begin, tiles)],
                targets[c].at[:, pl.ds(0, tiles)],
                out_sem.at[direction, c],
            )
            copy.start()
            stores.append(copy)
            begin += tiles
        copy = pltpu.make_async_copy(
            place_ref, targets[0].at[0, chunks[0]], out_sem.at[direction, count]
        )
        copy.start()
        stores.append(copy)
    for copy in stores:
        copy.wait()


def tables(place, select_ref, groups):
    parts = []
    for group in groups:
        angle = None
        for part in range(3):
            term = lax.dot_general(
                place,
                select_ref[part, group],
                (((0,), (0,)), ((), ())),
                preferred_element_type=jnp.float32,
            )
            angle = term if angle is None else angle + term
        parts.append(angle)
    angle = jnp.concatenate(parts, axis=0)
    return jnp.cos(angle), jnp.sin(angle)


def rotate(x, cosine, sine, turn):
    swapped = jnp.dot(x, turn, preferred_element_type=jnp.float32)
    return x.astype(jnp.float32) * cosine + swapped * sine


def attend(q, k, v, bias):
    scale = math.log2(math.e) / math.sqrt(HD)
    scores = lax.dot_general(q, k, (((1,), (1,)), ((), ())), preferred_element_type=jnp.float32)
    scores = scores * scale + bias
    top = jnp.max(scores, axis=1, keepdims=True)
    weight = jnp.exp2(scores - top)
    total = jnp.sum(weight, axis=1, keepdims=True)
    summed = jnp.dot(weight.astype(jnp.bfloat16), v, preferred_element_type=jnp.float32)
    return (summed * (1.0 / total)).astype(jnp.bfloat16)


def head_weights(w_block, scale_row):
    scaled = (w_block.astype(jnp.float32) * (1.0 + scale_row)).astype(jnp.bfloat16)
    zeros = jnp.zeros((HD - LATC, HD), jnp.bfloat16)
    first = jnp.concatenate([scaled, zeros], axis=0)
    row = lax.broadcasted_iota(jnp.int32, (HD, HD), 0)
    second = (row == LATC).astype(jnp.bfloat16)
    return jnp.concatenate([first, second], axis=1)


def contribution(attended, weights):
    wide = attended.astype(jnp.float32)
    squared = (wide * wide).astype(jnp.bfloat16)
    joined = jnp.concatenate([attended, squared], axis=1)
    return lax.dot_general(
        joined, weights, (((1,), (1,)), ((), ())), preferred_element_type=jnp.float32
    )


def local_kernel(
    scal_ref, place_ref, select_ref, turn_ref, seg_row_ref, seg_col_ref,
    q_ref, k_ref, v_ref, w_ref, mod_ref, turned_ref, acc_ref, cos_ref, sin_ref, bias_ref,
):
    head = pl.program_id(0)

    @pl.when(head == 0)
    def _():
        cosine, sine = tables(place_ref[...], select_ref, range(4))
        cos_ref[...] = cosine
        sin_ref[...] = sine
        same = seg_col_ref[...] == seg_row_ref[...]
        bias_ref[...] = jnp.where(same, 0.0, masked_score)
        acc_ref[...] = jnp.zeros_like(acc_ref)

    turn = turn_ref[...]
    turned_ref[0, 0] = rotate(q_ref[...], cos_ref[...], sin_ref[...], turn).astype(jnp.bfloat16)
    turned_ref[0, 1] = rotate(k_ref[...], cos_ref[...], sin_ref[...], turn).astype(jnp.bfloat16)
    turned_ref[0, 2] = v_ref[...]
    first = scal_ref[1]
    last = ROWS - scal_ref[3]
    start = jnp.minimum(first // HD * HD, ROWS // 2)
    narrow = last <= start + ROWS // 2
    weights = head_weights(w_ref[...], mod_ref[1:2, :])

    def run(begin, width):
        keys = turned_ref[0, 1, pl.ds(begin, width)]
        values = turned_ref[0, 2, pl.ds(begin, width)]
        for part in range(width // 128):
            rows = pl.ds(begin + part * 128, 128)
            bias = bias_ref[rows, pl.ds(begin, width)]
            attended = attend(turned_ref[0, 0, rows], keys, values, bias)
            acc_ref[rows] += contribution(attended, weights)

    @pl.when((first < last) & narrow)
    def _():
        run(pl.multiple_of(start, HD), ROWS // 2)

    @pl.when((first < last) & jnp.logical_not(narrow))
    def _():
        run(0, ROWS)


def cut_kernel(heads, chunks, c, *refs):
    final = c == len(chunks) - 1
    refs = list(refs)
    scal_ref, select_ref, turn_ref, w_ref, mod_ref, turned_ref = refs[:6]
    del refs[:6]
    here = [i for i in (c - 1, c) if i >= 0]
    sources = [refs[: len(here)], refs[len(here) : 2 * len(here)]]
    del refs[: 2 * len(here)]
    if c == 0:
        acc_ref, table_ref = refs[:2]
        del refs[:2]
    else:
        table_ref, before_ref = refs[:2]
        del refs[:2]
        if final:
            local_ref, own_ref, left_out, right_out, shift_ref = refs[:5]
            del refs[:5]
        else:
            acc_ref = refs.pop(0)
    if final:
        span, mine, recv, loc_sem, recv_sem, acc_ref = refs
    else:
        span, mine, recv, loc_sem, recv_sem = refs
    begins = [sum(chunks[:i]) for i in range(len(chunks) + 1)]
    base = begins[here[0]]
    loads = []
    for side in range(2):
        for i, index in enumerate(here):
            copy = pltpu.make_async_copy(
                sources[side][i].at[:, pl.ds(0, chunks[index])],
                recv.at[side, :, pl.ds(FAR + begins[index] - base, chunks[index])],
                recv_sem.at[side, i],
            )
            copy.start()
            loads.append(copy)
    if c == 0:
        place_copies = []
        for side in range(2):
            copy = pltpu.make_async_copy(
                sources[side][0].at[0, chunks[0]], recv.at[side, 0, 0], recv_sem.at[side, 2]
            )
            copy.start()
            place_copies.append(copy)
    a_low, b_low, n_low = scal_ref[0], scal_ref[1], scal_ref[2]
    a_high, b_high, n_high = scal_ref[3], scal_ref[4], scal_ref[5]
    ta_low = cdiv(a_low, TILE)
    tb_high = cdiv(b_high, TILE)

    def done(limit, tiles, total):
        if limit == 0:
            return jnp.int32(0)
        return jnp.where(tiles > 0, jnp.minimum(total, limit // jnp.maximum(tiles, 1)), 0)

    low_first = done(begins[c], ta_low, n_low)
    low_count = done(begins[c + 1], ta_low, n_low) - low_first
    high_first = done(begins[c], tb_high, heads - n_high)
    high_count = done(begins[c + 1], tb_high, heads - n_high) - high_first
    items = low_count + high_count

    def slot_of(i):
        return jnp.where(i < low_count, low_first + i, high_first + i - low_count)

    def head_of(i):
        return jnp.where(i < low_count, low_first + i, n_high + high_first + i - low_count)

    def fetch(i, buffer):
        return pltpu.make_async_copy(turned_ref.at[head_of(i)], mine.at[buffer], loc_sem.at[buffer])

    @pl.when(items > 0)
    def _():
        fetch(jnp.int32(0), 0).start()

    span[...] = jnp.zeros_like(span)
    if c == 0:
        acc_ref[...] = jnp.zeros_like(acc_ref)
        for side, copy in enumerate(place_copies):
            copy.wait()
            groups = range(1, 4) if side == 0 else range(3)
            cosine, sine = tables(recv[side, 0, 0], select_ref, groups)
            table_ref[side, 0] = cosine
            table_ref[side, 1] = sine
    else:
        acc_ref[...] = before_ref[...]
    for copy in loads:
        copy.wait()
    turn = turn_ref[...]

    def one(i, carry):
        buffer = lax.rem(i, 2)
        fetch(i, buffer).wait()

        @pl.when(i + 1 < items)
        def _():
            fetch(i + 1, 1 - buffer).start()

        side = (i >= low_count).astype(jnp.int32)
        is_low = side == 0
        slot = slot_of(i)
        head = head_of(i)
        a = jnp.where(is_low, a_low, a_high)
        b = jnp.where(is_low, b_low, b_high)
        ta, tb = cdiv(a, TILE), cdiv(b, TILE)
        offset = jnp.where(is_low, slot * ta + ta, slot * tb + FAR) - base
        row = lax.broadcasted_iota(jnp.int32, (REACH, HD), 0)
        keep = (row >= jnp.where(is_low, REACH - ta * TILE, 0)) & (
            row < jnp.where(is_low, REACH, tb * TILE)
        )
        cosine, sine = table_ref[side, 0], table_ref[side, 1]
        target = pl.ds(pl.multiple_of(jnp.where(is_low, ROWS - REACH, ROWS), 128), REACH)
        for j in range(3):
            x = recv[side, j, pl.ds(offset, FAR)].reshape(REACH, HD)
            if j < 2:
                x = rotate(x, cosine, sine, turn)
            else:
                x = x.astype(jnp.float32)
            span[j, target] = jnp.where(keep, x, 0.0).astype(jnp.bfloat16)
        for j in range(3):
            span[j, pl.ds(pl.multiple_of(jnp.where(is_low, ROWS, 0), ROWS), ROWS)] = mine[buffer, j]
        columns = pl.ds(pl.multiple_of(head * HD, HD), HD)
        weights = head_weights(w_ref[:, columns], mod_ref[1:2, columns])
        start = pl.multiple_of(ROWS - ta * TILE, TILE)
        extent = (ta + tb) * TILE

        def run(width):
            keys = span[1, pl.ds(start, width)]
            values = span[2, pl.ds(start, width)]
            lane = lax.broadcasted_iota(jnp.int32, (1, width), 1)
            valid = (lane >= ta * TILE - a) & (lane < ta * TILE + b)
            bias = jnp.where(valid, 0.0, masked_score)
            for part in range(width // 128):
                rows = pl.ds(pl.multiple_of(start + part * 128, TILE), 128)
                attended = attend(span[0, rows], keys, values, bias)
                acc_ref[side, rows] += contribution(attended, weights)

        below = 0
        for width in (256, 384, 512, 640):

            @pl.when((extent > below) & (extent <= width))
            def _(width=width):
                run(width)

            below = width
        return carry

    lax.fori_loop(0, items, one, 0)
    if final:
        row = lax.broadcasted_iota(jnp.int32, (ROWS, HD), 0)
        own = jnp.where(row < b_low, acc_ref[0, ROWS : 2 * ROWS], 0.0)
        own = own + jnp.where(row >= ROWS - a_high, acc_ref[1, 0:ROWS], 0.0)
        own = own + jnp.where((row >= b_low) & (row < ROWS - a_high), local_ref[...], 0.0)
        own_ref[...] = own.T[:ACCR]
        row = lax.broadcasted_iota(jnp.int32, (REACH, HD), 0)
        back = jnp.where(row >= REACH - a_low, acc_ref[0, ROWS - REACH : ROWS], 0.0)
        left_out[...] = back.T[:ACCR]
        back = jnp.where(row < b_high, acc_ref[1, ROWS : ROWS + REACH], 0.0)
        right_out[...] = back.T[:ACCR]
        shift = jnp.sum(w_ref[...].astype(jnp.float32) * mod_ref[0:1, :], axis=1, keepdims=True)
        shift_ref[...] = jnp.broadcast_to(shift, (LATC, HD))


def finish_kernel(
    features, ring, own_ref, left_ref, right_ref, shift_ref, guide_ref, out_ref,
    from_left, from_right, velocity, other, send_sem, recv_sem,
):
    me = lax.axis_index("req")
    parity = lax.axis_index("cfg")
    left, right = lax.rem(me + ring - 1, ring), lax.rem(me + 1, ring)
    partner = {"cfg": 1 - parity}
    barrier = pltpu.get_barrier_semaphore()
    for target in ({"req": left}, {"req": right}, partner):
        pl.semaphore_signal(barrier, inc=1, device_id=target, device_id_type=MESH)
    pl.semaphore_wait(barrier, 3)
    to_left = pltpu.make_async_remote_copy(
        left_ref, from_right, send_sem.at[0], recv_sem.at[0],
        device_id={"req": left}, device_id_type=MESH,
    )
    to_left.start()
    to_right = pltpu.make_async_remote_copy(
        right_ref, from_left, send_sem.at[1], recv_sem.at[1],
        device_id={"req": right}, device_id_type=MESH,
    )
    to_right.start()
    to_left.wait()
    to_right.wait()
    none = jnp.zeros((ACCR, ROWS - REACH), jnp.float32)
    total = own_ref[...]
    total = total + jnp.concatenate([none, from_right[...]], axis=1)
    total = total + jnp.concatenate([from_left[...], none], axis=1)
    inverse = lax.rsqrt(total[LATC : LATC + 1] * (1.0 / features) + 1e-06)
    velocity[...] = total[:LATC] * inverse + shift_ref[:, 0:1]
    half = LATC // 2
    give = pltpu.make_async_remote_copy(
        velocity.at[pl.ds(pl.multiple_of((1 - parity) * half, half), half)],
        other, send_sem.at[2], recv_sem.at[2], device_id=partner, device_id_type=MESH,
    )
    give.start()
    kept = velocity[pl.ds(pl.multiple_of(parity * half, half), half)]
    give.wait()
    theirs = other[...]
    conditional = jnp.where(parity == 0, kept, theirs)
    unconditional = jnp.where(parity == 0, theirs, kept)
    out_ref[...] = unconditional + guide_ref[0] * (conditional - unconditional)


def moved(value, step, ring):
    return lax.ppermute(value, "req", [(i, (i + step) % ring) for i in range(ring)])


def per_device(
    query_rows, key_rows, value_rows, positions, latents, w_head, modulation, guide_scale,
    step_sizes, lengths,
):
    features = query_rows.shape[2]
    heads = features // HD
    ring = lax.axis_size("req")
    chunks = chunk_tiles(heads)
    count = len(chunks)
    bf16, f32 = jnp.bfloat16, jnp.float32
    sized = jax.ShapeDtypeStruct
    q, k, v = query_rows[0], key_rows[0], value_rows[0]

    def tiled(x):
        return x.reshape(TILES, TILE, features)

    shapes = [sized((3, t + (i == 0), TILE, HD), bf16) for i, t in enumerate(chunks)]
    packed_tiles = sum(chunks) + FAR
    outs = pl.pallas_call(
        functools.partial(pack_kernel, heads, chunks),
        out_shape=[sized((8,), jnp.int32), sized((TILE, HD), bf16)] + shapes + shapes,
        in_specs=[SMEM, VMEM, ANY, ANY, ANY],
        out_specs=[SMEM, VMEM] + [ANY] * (2 * count),
        scratch_shapes=[
            pltpu.VMEM((3, TILES + FAR, TILE, features), bf16),
            pltpu.VMEM((2, 3, packed_tiles, TILE, HD), bf16),
            pltpu.SemaphoreType.DMA((4, 3)),
            pltpu.SemaphoreType.DMA((2, count + 1)),
        ],
        name="pack",
    )(lengths, positions, tiled(q), tiled(k), tiled(v))
    scal, place = outs[:2]
    to_right, to_left = outs[2 : 2 + count], outs[2 + count :]
    from_left = []
    from_right = []
    for c in range(count):
        from_left.append(moved(to_right[c], 1, ring))
        from_right.append(moved(to_left[c], -1, ring))

    video_ends = jnp.cumsum(lengths)
    first_row = lax.axis_index("req") * ROWS
    rows_here = first_row + jnp.arange(ROWS, dtype=jnp.int32)
    videos = jnp.sum((video_ends[:, None] <= rows_here[None, :]).astype(jnp.int32), axis=0)
    chosen = videos[None, :] == jnp.arange(step_sizes.shape[0], dtype=jnp.int32)[:, None]
    steps = jnp.sum(jnp.where(chosen, step_sizes[:, None], 0.0), axis=0)

    select = jnp.asarray(selector())
    turn = jnp.asarray(turner())
    w_turned = w_head.T
    pair_ops = ROWS * ROWS * HD * 4
    turned, local_acc = pl.pallas_call(
        local_kernel,
        grid=(heads,),
        out_shape=[sized((heads, 3, ROWS, HD), bf16), sized((ROWS, HD), f32)],
        in_specs=[
            SMEM,
            VMEM,
            VMEM,
            VMEM,
            pl.BlockSpec((1, ROWS), lambda h: (0, 0)),
            pl.BlockSpec((ROWS, 1), lambda h: (0, 0)),
            pl.BlockSpec((ROWS, HD), lambda h: (0, h)),
            pl.BlockSpec((ROWS, HD), lambda h: (0, h)),
            pl.BlockSpec((ROWS, HD), lambda h: (0, h)),
            pl.BlockSpec((LATC, HD), lambda h: (0, h)),
            pl.BlockSpec((2, HD), lambda h: (0, h)),
        ],
        out_specs=[
            pl.BlockSpec((1, 3, ROWS, HD), lambda h: (h, 0, 0, 0)),
            pl.BlockSpec((ROWS, HD), lambda h: (0, 0)),
        ],
        scratch_shapes=[
            pltpu.VMEM((ROWS, HD), f32),
            pltpu.VMEM((ROWS, HD), f32),
            pltpu.VMEM((ROWS, ROWS), f32),
        ],
        cost_estimate=pl.CostEstimate(
            flops=heads * pair_ops, bytes_accessed=6 * ROWS * features * 2, transcendentals=0
        ),
        name="local",
    )(
        scal, place, select, turn, videos[None, :], videos[:, None], q, k, v, w_turned, modulation
    )

    acc = table = None
    for c in range(count):
        final = c == count - 1
        here = [i for i in (c - 1, c) if i >= 0]
        operands = [scal, select, turn, w_turned, modulation, turned]
        specs = [SMEM, VMEM, VMEM, VMEM, VMEM, ANY]
        operands += [from_left[i] for i in here] + [from_right[i] for i in here]
        specs += [ANY] * (2 * len(here))
        if c > 0:
            operands += [table, acc]
            specs += [VMEM, VMEM]
        acc_shape = sized((2, SPAN, HD), f32)
        if final:
            operands.append(local_acc)
            specs.append(VMEM)
            out_shape = [
                sized((ACCR, ROWS), f32),
                sized((ACCR, REACH), f32),
                sized((ACCR, REACH), f32),
                sized((LATC, HD), f32),
            ]
        elif c == 0:
            out_shape = [acc_shape, sized((2, 2, REACH, HD), f32)]
        else:
            out_shape = [acc_shape]
        scratch = [
            pltpu.VMEM((3, SPAN, HD), bf16),
            pltpu.VMEM((2, 3, ROWS, HD), bf16),
            pltpu.VMEM((2, 3, 2 * FAR + sum(chunks[i] for i in here), TILE, HD), bf16),
            pltpu.SemaphoreType.DMA((2,)),
            pltpu.SemaphoreType.DMA((2, 3)),
        ]
        if final:
            scratch.append(pltpu.VMEM((2, SPAN, HD), f32))
        results = pl.pallas_call(
            functools.partial(cut_kernel, heads, chunks, c),
            out_shape=out_shape,
            in_specs=specs,
            out_specs=[VMEM] * len(out_shape),
            scratch_shapes=scratch,
            cost_estimate=pl.CostEstimate(
                flops=heads * pair_ops // count, bytes_accessed=4 << 20, transcendentals=0
            ),
        )(*operands)
        if final:
            own, back_left, back_right, shift = results
        elif c == 0:
            acc, table = results
        else:
            (acc,) = results

    guided = pl.pallas_call(
        functools.partial(finish_kernel, features, ring),
        out_shape=sized((LATC // 2, ROWS), f32),
        in_specs=[VMEM, VMEM, VMEM, VMEM, SMEM],
        out_specs=VMEM,
        scratch_shapes=[
            pltpu.VMEM((ACCR, REACH), f32),
            pltpu.VMEM((ACCR, REACH), f32),
            pltpu.VMEM((LATC, ROWS), f32),
            pltpu.VMEM((LATC // 2, ROWS), f32),
            pltpu.SemaphoreType.DMA((3,)),
            pltpu.SemaphoreType.DMA((3,)),
        ],
        compiler_params=pltpu.CompilerParams(collective_id=0, has_side_effects=True),
        name="finish",
    )(own, back_left, back_right, shift, guide_scale)
    return (latents.T + steps[None, :] * guided).T


def solution(mesh):
    in_specs = (
        P("cfg", "req", None),
        P("cfg", "req", None),
        P("cfg", "req", None),
        P(None, "req"),
        P("req", "cfg"),
        P(),
        P(),
        P(),
        P(),
        P(),
    )
    return jax.shard_map(
        per_device, mesh=mesh, in_specs=in_specs, out_specs=P("req", "cfg"), check_vma=False
    )
```

```python
import functools
import math

import jax
import jax.numpy as jnp
import numpy as np
from jax import lax
from jax.experimental import pallas as pl
from jax.experimental.pallas import tpu as pltpu
from jax.sharding import PartitionSpec as P

HD = 128
ROWS = 512
LATC = 64
TILE = 16
TILES = ROWS // TILE
FAR = 24
REACH = FAR * TILE
SPAN = 2 * ROWS + 128
ACCR = 72
masked_score = -1e30
score_scale = math.log2(math.e) / math.sqrt(HD)
rope_theta = 10000.0
MESH = pl.DeviceIdType.MESH
SMEM = pl.BlockSpec(memory_space=pltpu.SMEM)
VMEM = pl.BlockSpec(memory_space=pltpu.VMEM)
ANY = pl.BlockSpec(memory_space=pl.ANY)


def share_static(ta, tb, heads):
    if ta > FAR:
        return 0
    if tb > FAR:
        return heads
    costs = [max(n * ta, (heads - n) * tb) for n in range(heads + 1)]
    return costs.index(min(costs))


def capacity(heads):
    most = 0
    for ta in range(1, TILES + 1):
        for tb in range(1, TILES + 2 - ta):
            n = share_static(ta, tb, heads)
            most = max(most, n * ta, (heads - n) * tb)
    return most


def chunking(heads):
    cap = capacity(heads)
    count = max(1, cap // 34)
    return cdiv(cap, count), count


def share(ta, tb, heads):
    best = heads * tb
    chosen = jnp.int32(0)
    for n in range(1, heads + 1):
        cost = jnp.maximum(n * ta, (heads - n) * tb)
        better = cost < best
        best = jnp.where(better, cost, best)
        chosen = jnp.where(better, n, chosen)
    chosen = jnp.where(tb > FAR, heads, chosen)
    return jnp.where(ta > FAR, 0, chosen)


def selector():
    pair_total = HD // 2
    side = HD // 6
    time = pair_total - 2 * side
    axis = np.array([0] * time + [1] * side + [2] * side)
    local = np.array(list(range(time)) + list(range(side)) * 2, np.float32)
    pairs = np.array([time] * time + [side] * (2 * side), np.float32)
    frequency = np.exp(-(local / pairs) * np.float32(math.log(rope_theta))).astype(np.float32)
    table = np.zeros((4, TILE, HD), np.float32)
    for group in range(4):
        for lane in range(HD):
            table[group, axis[lane // 2] * 4 + group, lane] = frequency[lane // 2]
    parts = []
    rest = table
    for _ in range(3):
        part = rest.astype(jnp.bfloat16)
        parts.append(part)
        rest = rest - part.astype(np.float32)
    return np.stack(parts)


def turner():
    table = np.zeros((2 * HD, 2 * HD), np.float32)
    for pair in range(HD):
        table[2 * pair + 1, 2 * pair] = -1.0
        table[2 * pair, 2 * pair + 1] = 1.0
    return table.astype(jnp.bfloat16)


def cdiv(value, unit):
    return (value + unit - 1) // unit


def tables(place, select_ref, groups):
    parts = []
    for group in groups:
        angle = None
        for part in range(3):
            term = lax.dot_general(
                place,
                select_ref[part, group],
                (((0,), (0,)), ((), ())),
                preferred_element_type=jnp.float32,
            )
            angle = term if angle is None else angle + term
        parts.append(angle)
    angle = jnp.concatenate(parts, axis=0)
    return jnp.cos(angle), jnp.sin(angle)


def rotate(q, k, cosine, sine, turn):
    both = jnp.concatenate([q, k], axis=1)
    swapped = jnp.dot(both, turn, preferred_element_type=jnp.float32)
    return (
        q.astype(jnp.float32) * cosine + swapped[:, :HD] * sine,
        k.astype(jnp.float32) * cosine + swapped[:, HD:] * sine,
    )


def attend(q, k, v, bias):
    scores = lax.dot_general(q, k, (((1,), (1,)), ((), ())), preferred_element_type=jnp.float32)
    scores = scores + bias
    top = jnp.max(scores, axis=1, keepdims=True)
    weight = jnp.exp2((scores - top) * score_scale).astype(jnp.bfloat16)
    widened = jnp.concatenate([v, jnp.ones(v.shape, jnp.bfloat16)], axis=1)
    summed = jnp.dot(weight, widened, preferred_element_type=jnp.float32)
    return (summed[:, :HD] * (1.0 / summed[:, HD:])).astype(jnp.bfloat16)


def head_weights(w_block, scale_row):
    scaled = (w_block.astype(jnp.float32) * (1.0 + scale_row)).astype(jnp.bfloat16)
    return jnp.concatenate([scaled, jnp.zeros_like(scaled)], axis=0)


def project(attended, weights):
    return lax.dot_general(
        attended, weights, (((1,), (1,)), ((), ())), preferred_element_type=jnp.float32
    )


def squares(attended):
    wide = attended.astype(jnp.float32)
    return wide * wide


def with_squares(acc, squared):
    lane = lax.broadcasted_iota(jnp.int32, acc.shape, 1)
    return jnp.where(lane == LATC, jnp.sum(squared, axis=1, keepdims=True), acc)


def pack_kernel(
    heads, unit, count, lens_ref, pos_ref, q_ref, k_ref, v_ref, scal_ref, place, out_ref,
    rows_in, packed, in_sem, out_sem,
):
    me = lax.axis_index("req")
    groups = 4 if heads % 4 == 0 else 1
    width = heads // groups * HD
    loads = []
    for group in range(groups):
        columns = pl.ds(group * width, width)
        for j, source in enumerate((q_ref, k_ref, v_ref)):
            copy = pltpu.make_async_copy(
                source.at[:, :, columns], rows_in.at[j, :, :, columns], in_sem.at[group, j]
            )
            copy.start()
            loads.append(copy)
    low = me * ROWS
    high = low + ROWS

    def scan(i, carry):
        end, start_low, end_low, start_high, end_high = carry
        start = end
        end = start + lens_ref[i]
        before_low = start < low
        before_high = start < high
        return (
            end,
            jnp.where(before_low, start, start_low),
            jnp.where(before_low, end, end_low),
            jnp.where(before_high, start, start_high),
            jnp.where(before_high, end, end_high),
        )

    zero = jnp.int32(0)
    _, start_low, end_low, start_high, end_high = lax.fori_loop(
        0, lens_ref.shape[0], scan, (zero, low, low, high, high), unroll=8
    )
    cut_low = end_low > low
    cut_high = end_high > high
    a_low = jnp.where(cut_low, low - start_low, 0)
    b_low = jnp.where(cut_low, end_low - low, 0)
    a_high = jnp.where(cut_high, high - start_high, 0)
    b_high = jnp.where(cut_high, end_high - high, 0)
    n_low = share(cdiv(a_low, TILE), cdiv(b_low, TILE), heads)
    n_high = share(cdiv(a_high, TILE), cdiv(b_high, TILE), heads)
    for i, value in enumerate((a_low, b_low, n_low, a_high, b_high, n_high, zero, zero)):
        scal_ref[i] = value

    placed = pos_ref[...].astype(jnp.float32)
    pieces = [placed[a : a + 1, g * HD : (g + 1) * HD] for a in range(3) for g in range(4)]
    pieces.append(jnp.zeros((TILE - 12, HD), jnp.float32))
    place[...] = jnp.concatenate(pieces, axis=0).astype(jnp.bfloat16)
    for copy in loads:
        copy.wait()
    ta, tb = cdiv(a_high, TILE), cdiv(b_low, TILE)

    def pack(t, carry):
        head_r, tile_r, head_l, tile_l = carry
        columns = pl.ds(pl.multiple_of(head_r * HD, HD), HD)
        source = jnp.minimum(TILES - ta + tile_r, TILES - 1)
        for j in range(3):
            packed[0, j, t] = rows_in[j, source, :, columns]
        columns = pl.ds(pl.multiple_of(head_l * HD, HD), HD)
        for j in range(3):
            packed[1, j, t] = rows_in[j, tile_l, :, columns]
        over_r = tile_r + 1 >= ta
        over_l = tile_l + 1 >= tb
        return (
            jnp.minimum(jnp.where(over_r, head_r + 1, head_r), heads - 1),
            jnp.where(over_r, 0, tile_r + 1),
            jnp.minimum(jnp.where(over_l, head_l + 1, head_l), heads - 1),
            jnp.where(over_l, 0, tile_l + 1),
        )

    carry = (zero, zero, jnp.minimum(n_low, heads - 1), zero)
    stores = []
    for c in range(count):
        carry = lax.fori_loop(c * unit, (c + 1) * unit, pack, carry, unroll=2)
        chunk = pl.ds(c * unit, unit)
        copy = pltpu.make_async_copy(packed.at[:, :, chunk], out_ref.at[:, :, chunk], out_sem.at[c])
        copy.start()
        stores.append(copy)
    for copy in stores:
        copy.wait()


def main_kernel(
    heads, ring, unit, count, lens_ref, step_ref, place, packed, select_ref, turn_ref, w_ref,
    mod_ref, q_ref, k_ref, v_ref, steps_ref, table_ref, acc_ref, turned_ref, recv_ref,
    rows_in, places, cos_ref, sin_ref, bias_ref, square_ref, mine,
    in_sem, send_sem, recv_sem, place_send, place_recv, out_sem,
):
    me = lax.axis_index("req")
    left, right = lax.rem(me + ring - 1, ring), lax.rem(me + 1, ring)
    barrier = pltpu.get_barrier_semaphore()
    for target in (left, right):
        pl.semaphore_signal(barrier, inc=1, device_id={"req": target}, device_id_type=MESH)
    pl.semaphore_wait(barrier, 2)
    sends = []
    for direction, target in ((0, right), (1, left)):
        copy = pltpu.make_async_remote_copy(
            place, places.at[direction], place_send.at[direction],
            place_recv.at[direction], device_id={"req": target}, device_id_type=MESH,
        )
        copy.start()
        sends.append(copy)
    for c in range(count):
        chunk = pl.ds(c * unit, unit)
        for direction, target in ((0, right), (1, left)):
            copy = pltpu.make_async_remote_copy(
                packed.at[direction, :, chunk], recv_ref.at[direction, :, chunk],
                send_sem.at[direction, c], recv_sem.at[direction, c],
                device_id={"req": target}, device_id_type=MESH,
            )
            copy.start()
            sends.append(copy)
    groups = 4 if heads % 4 == 0 else 1
    width = heads // groups * HD
    loads = []
    for group in range(groups):
        columns = pl.ds(group * width, width)
        for j, source in enumerate((q_ref, k_ref, v_ref)):
            copy = pltpu.make_async_copy(
                source.at[:, :, columns], rows_in.at[j, :, :, columns], in_sem.at[group, j]
            )
            copy.start()
            loads.append(copy)
    low = me * ROWS
    zero = jnp.int32(0)
    lane = lax.broadcasted_iota(jnp.int32, (1, ROWS), 1) + low

    def label(i, carry):
        end, video, step = carry
        end = end + lens_ref[i]
        past = lane >= end
        video = video + past.astype(jnp.int32)
        following = step_ref[jnp.minimum(i + 1, lens_ref.shape[0] - 1)]
        return end, video, jnp.where(past, following, step)

    start = jnp.full((1, ROWS), step_ref[0], jnp.float32)
    _, video, step = lax.fori_loop(
        0, lens_ref.shape[0], label, (zero, jnp.zeros((1, ROWS), jnp.int32), start), unroll=8
    )
    steps_ref[...] = step
    tall = jnp.broadcast_to(video.astype(jnp.float32), (HD, ROWS)).T
    for part in range(ROWS // HD):
        wide = jnp.broadcast_to(
            video[:, part * HD : (part + 1) * HD].astype(jnp.float32), (ROWS, HD)
        )
        bias_ref[:, part * HD : (part + 1) * HD] = jnp.where(tall == wide, 0.0, masked_score)
    cosine, sine = tables(place[...], select_ref, range(4))
    cos_ref[...] = cosine
    sin_ref[...] = sine
    acc_ref[...] = jnp.zeros_like(acc_ref)
    square_ref[...] = jnp.zeros_like(square_ref)
    turn = turn_ref[...]
    for copy in loads:
        copy.wait()

    def keep(head, slot):
        return pltpu.make_async_copy(mine.at[slot], turned_ref.at[head], out_sem.at[slot])

    def one(head, slot):
        columns = pl.ds(pl.multiple_of(head * HD, HD), HD)
        q = rows_in[0, :, :, columns].reshape(ROWS, HD)
        k = rows_in[1, :, :, columns].reshape(ROWS, HD)
        q, k = rotate(q, k, cos_ref[...], sin_ref[...], turn)
        mine[slot, 0] = q.astype(jnp.bfloat16)
        mine[slot, 1] = k.astype(jnp.bfloat16)
        mine[slot, 2] = rows_in[2, :, :, columns].reshape(ROWS, HD)
        keep(head, slot).start()
        attended = attend(mine[slot, 0], mine[slot, 1], mine[slot, 2], bias_ref[...])
        square_ref[...] += squares(attended)
        return attended, head_weights(w_ref[:, columns], mod_ref[1:2, columns])

    def couple(pair, carry):
        first, second = (one(2 * pair + slot, slot) for slot in range(2))
        attended = jnp.concatenate([first[0], second[0]], axis=1)
        acc_ref[...] += project(attended, jnp.concatenate([first[1], second[1]], axis=1))
        for slot in range(2):
            keep(2 * pair + slot, slot).wait()
        return carry

    lax.fori_loop(0, heads // 2, couple, 0)
    acc_ref[...] = with_squares(acc_ref[...], square_ref[...])
    for side in range(2):
        sends[side].wait()
        groups = range(1, 4) if side == 0 else range(3)
        cosine, sine = tables(places[side], select_ref, groups)
        table_ref[side, 0] = cosine
        table_ref[side, 1] = sine
    for copy in sends[2:]:
        copy.wait()


def cut_kernel(
    heads, unit, count, scal_ref, table_ref, local_ref, turn_ref, w_ref, mod_ref,
    turned_ref, recv_ref, own_ref, left_out, right_out, shift_ref,
    span, mine, recv, acc_ref, square_ref, loc_sem, recv_sem,
):
    loads = []
    for side in range(2):
        copy = pltpu.make_async_copy(
            recv_ref.at[side], recv.at[side, :, pl.ds(FAR, unit * count)], recv_sem.at[side]
        )
        copy.start()
        loads.append(copy)
    a_low, b_low, n_low = scal_ref[0], scal_ref[1], scal_ref[2]
    a_high, b_high, n_high = scal_ref[3], scal_ref[4], scal_ref[5]
    low_count = jnp.where(a_low > 0, n_low, 0)
    high_count = jnp.where(a_high > 0, heads - n_high, 0)
    items = low_count + high_count

    def head_of(i):
        return jnp.where(i < low_count, i, n_high + i - low_count)

    def fetch(i, buffer):
        return pltpu.make_async_copy(turned_ref.at[head_of(i)], mine.at[buffer], loc_sem.at[buffer])

    @pl.when(items > 0)
    def _():
        fetch(jnp.int32(0), 0).start()

    span[...] = jnp.zeros_like(span)
    acc_ref[...] = jnp.zeros_like(acc_ref)
    square_ref[...] = jnp.zeros_like(square_ref)
    turn = turn_ref[...]
    for copy in loads:
        copy.wait()

    def one(i, carry):
        buffer = lax.rem(i, 2)
        fetch(i, buffer).wait()

        @pl.when(i + 1 < items)
        def _():
            fetch(i + 1, 1 - buffer).start()

        side = (i >= low_count).astype(jnp.int32)
        is_low = side == 0
        slot = jnp.where(is_low, i, i - low_count)
        head = head_of(i)
        a = jnp.where(is_low, a_low, a_high)
        b = jnp.where(is_low, b_low, b_high)
        ta, tb = cdiv(a, TILE), cdiv(b, TILE)
        offset = jnp.where(is_low, slot * ta + ta, slot * tb + FAR)
        row = lax.broadcasted_iota(jnp.int32, (REACH, HD), 0)
        keep = (row >= jnp.where(is_low, REACH - ta * TILE, 0)) & (
            row < jnp.where(is_low, REACH, tb * TILE)
        )
        cosine, sine = table_ref[side, 0], table_ref[side, 1]
        target = pl.ds(pl.multiple_of(jnp.where(is_low, ROWS - REACH, ROWS), 128), REACH)
        q, k, v = (recv[side, j, pl.ds(offset, FAR)].reshape(REACH, HD) for j in range(3))
        q, k = rotate(q, k, cosine, sine, turn)
        for j, x in enumerate((q, k, v.astype(jnp.float32))):
            span[j, target] = jnp.where(keep, x, 0.0).astype(jnp.bfloat16)
        for j in range(3):
            span[j, pl.ds(pl.multiple_of(jnp.where(is_low, ROWS, 0), ROWS), ROWS)] = mine[buffer, j]
        columns = pl.ds(pl.multiple_of(head * HD, HD), HD)
        weights = head_weights(w_ref[:, columns], mod_ref[1:2, columns])
        start = pl.multiple_of(ROWS - ta * TILE, TILE)
        extent = (ta + tb) * TILE

        def run(width):
            lane = lax.broadcasted_iota(jnp.int32, (1, width), 1)
            valid = (lane >= ta * TILE - a) & (lane < ta * TILE + b)
            bias = jnp.where(valid, 0.0, masked_score)

            rows = pl.ds(start, width)
            attended = attend(span[0, rows], span[1, rows], span[2, rows], bias)
            acc_ref[side, rows] += project(attended, weights)
            square_ref[side, rows] += squares(attended)

        below = 0
        for width in (128, 256, 384, 512, 528):

            @pl.when((extent > below) & (extent <= width))
            def _(width=width):
                run(width)

            below = width
        return carry

    lax.fori_loop(0, items, one, 0)
    for side in range(2):
        acc_ref[side] = with_squares(acc_ref[side], square_ref[side])
    row = lax.broadcasted_iota(jnp.int32, (ROWS, HD), 0)
    own = jnp.where(row < b_low, acc_ref[0, ROWS : 2 * ROWS], 0.0)
    own = own + jnp.where(row >= ROWS - a_high, acc_ref[1, 0:ROWS], 0.0)
    own = own + jnp.where((row >= b_low) & (row < ROWS - a_high), local_ref[...], 0.0)
    own_ref[...] = own.T[:ACCR]
    row = lax.broadcasted_iota(jnp.int32, (REACH, HD), 0)
    back = jnp.where(row >= REACH - a_low, acc_ref[0, ROWS - REACH : ROWS], 0.0)
    left_out[...] = back.T[:ACCR]
    back = jnp.where(row < b_high, acc_ref[1, ROWS : ROWS + REACH], 0.0)
    right_out[...] = back.T[:ACCR]
    shift = jnp.sum(w_ref[...].astype(jnp.float32) * mod_ref[0:1, :], axis=1, keepdims=True)
    shift_ref[...] = jnp.broadcast_to(shift, (LATC, HD))


def finish_kernel(
    features, ring, own_ref, left_ref, right_ref, shift_ref, guide_ref, out_ref,
    from_left, from_right, velocity, other, send_sem, recv_sem,
):
    me = lax.axis_index("req")
    parity = lax.axis_index("cfg")
    left, right = lax.rem(me + ring - 1, ring), lax.rem(me + 1, ring)
    partner = {"cfg": 1 - parity}
    barrier = pltpu.get_barrier_semaphore()
    for target in ({"req": left}, {"req": right}, partner):
        pl.semaphore_signal(barrier, inc=1, device_id=target, device_id_type=MESH)
    pl.semaphore_wait(barrier, 3)
    to_left = pltpu.make_async_remote_copy(
        left_ref, from_right, send_sem.at[0], recv_sem.at[0],
        device_id={"req": left}, device_id_type=MESH,
    )
    to_left.start()
    to_right = pltpu.make_async_remote_copy(
        right_ref, from_left, send_sem.at[1], recv_sem.at[1],
        device_id={"req": right}, device_id_type=MESH,
    )
    to_right.start()
    to_left.wait()
    to_right.wait()
    none = jnp.zeros((ACCR, ROWS - REACH), jnp.float32)
    total = own_ref[...]
    total = total + jnp.concatenate([none, from_right[...]], axis=1)
    total = total + jnp.concatenate([from_left[...], none], axis=1)
    inverse = lax.rsqrt(total[LATC : LATC + 1] * (1.0 / features) + 1e-06)
    velocity[...] = total[:LATC] * inverse + shift_ref[:, 0:1]
    half = LATC // 2
    give = pltpu.make_async_remote_copy(
        velocity.at[pl.ds(pl.multiple_of((1 - parity) * half, half), half)],
        other, send_sem.at[2], recv_sem.at[2], device_id=partner, device_id_type=MESH,
    )
    give.start()
    kept = velocity[pl.ds(pl.multiple_of(parity * half, half), half)]
    give.wait()
    theirs = other[...]
    conditional = jnp.where(parity == 0, kept, theirs)
    unconditional = jnp.where(parity == 0, theirs, kept)
    out_ref[...] = unconditional + guide_ref[0] * (conditional - unconditional)


def per_device(
    query_rows, key_rows, value_rows, positions, latents, w_head, modulation, guide_scale,
    step_sizes, lengths,
):
    features = query_rows.shape[2]
    heads = features // HD
    ring = lax.axis_size("req")
    unit, count = chunking(heads)
    bf16, f32 = jnp.bfloat16, jnp.float32
    sized = jax.ShapeDtypeStruct
    tiled = [
        x.reshape(TILES, TILE, features) for x in (query_rows, key_rows, value_rows)
    ]
    turn = jnp.asarray(turner())
    w_turned = w_head.T
    scal, place, packed = pl.pallas_call(
        functools.partial(pack_kernel, heads, unit, count),
        out_shape=[
            sized((8,), jnp.int32),
            sized((TILE, HD), bf16),
            sized((2, 3, unit * count, TILE, HD), bf16),
        ],
        in_specs=[SMEM, VMEM] + [ANY] * 3,
        out_specs=[SMEM, VMEM, ANY],
        scratch_shapes=[
            pltpu.VMEM((3, TILES, TILE, features), bf16),
            pltpu.VMEM((2, 3, unit * count, TILE, HD), bf16),
            pltpu.SemaphoreType.DMA((4, 3)),
            pltpu.SemaphoreType.DMA((count,)),
        ],
        name="pack",
    )(lengths, positions, *tiled)
    steps, table, local_acc, turned, recv = pl.pallas_call(
        functools.partial(main_kernel, heads, ring, unit, count),
        out_shape=[
            sized((1, ROWS), f32),
            sized((2, 2, REACH, HD), f32),
            sized((ROWS, HD), f32),
            sized((heads, 3, ROWS, HD), bf16),
            sized((2, 3, unit * count, TILE, HD), bf16),
        ],
        in_specs=[SMEM, SMEM, VMEM, ANY] + [VMEM] * 4 + [ANY] * 3,
        out_specs=[VMEM, VMEM, VMEM, ANY, ANY],
        scratch_shapes=[
            pltpu.VMEM((3, TILES, TILE, features), bf16),
            pltpu.VMEM((2, TILE, HD), bf16),
            pltpu.VMEM((ROWS, HD), f32),
            pltpu.VMEM((ROWS, HD), f32),
            pltpu.VMEM((ROWS, ROWS), f32),
            pltpu.VMEM((ROWS, HD), f32),
            pltpu.VMEM((2, 3, ROWS, HD), bf16),
            pltpu.SemaphoreType.DMA((4, 3)),
            pltpu.SemaphoreType.DMA((2, count)),
            pltpu.SemaphoreType.DMA((2, count)),
            pltpu.SemaphoreType.DMA((2,)),
            pltpu.SemaphoreType.DMA((2,)),
            pltpu.SemaphoreType.DMA((2,)),
        ],
        compiler_params=pltpu.CompilerParams(collective_id=1, has_side_effects=True),
        name="main",
    )(
        lengths, step_sizes, place, packed, jnp.asarray(selector()), turn, w_turned, modulation,
        *tiled,
    )
    own, back_left, back_right, shift = pl.pallas_call(
        functools.partial(cut_kernel, heads, unit, count),
        out_shape=[
            sized((ACCR, ROWS), f32),
            sized((ACCR, REACH), f32),
            sized((ACCR, REACH), f32),
            sized((LATC, HD), f32),
        ],
        in_specs=[SMEM] + [VMEM] * 5 + [ANY] * 2,
        out_specs=[VMEM] * 4,
        scratch_shapes=[
            pltpu.VMEM((3, SPAN, HD), bf16),
            pltpu.VMEM((2, 3, ROWS, HD), bf16),
            pltpu.VMEM((2, 3, 2 * FAR + unit * count, TILE, HD), bf16),
            pltpu.VMEM((2, SPAN, HD), f32),
            pltpu.VMEM((2, SPAN, HD), f32),
            pltpu.SemaphoreType.DMA((2,)),
            pltpu.SemaphoreType.DMA((2,)),
        ],
        name="cut",
    )(scal, table, local_acc, turn, w_turned, modulation, turned, recv)
    guided = pl.pallas_call(
        functools.partial(finish_kernel, features, ring),
        out_shape=sized((LATC // 2, ROWS), f32),
        in_specs=[VMEM, VMEM, VMEM, VMEM, SMEM],
        out_specs=VMEM,
        scratch_shapes=[
            pltpu.VMEM((ACCR, REACH), f32),
            pltpu.VMEM((ACCR, REACH), f32),
            pltpu.VMEM((LATC, ROWS), f32),
            pltpu.VMEM((LATC // 2, ROWS), f32),
            pltpu.SemaphoreType.DMA((3,)),
            pltpu.SemaphoreType.DMA((3,)),
        ],
        compiler_params=pltpu.CompilerParams(collective_id=0, has_side_effects=True),
        name="finish",
    )(own, back_left, back_right, shift, guide_scale)
    return (latents.T + steps * guided).T


def solution(mesh):
    in_specs = (
        P("cfg", "req", None),
        P("cfg", "req", None),
        P("cfg", "req", None),
        P(None, "req"),
        P("req", "cfg"),
        P(),
        P(),
        P(),
        P(),
        P(),
    )
    return jax.shard_map(
        per_device, mesh=mesh, in_specs=in_specs, out_specs=P("req", "cfg"), check_vma=False
    )
```

```python
import functools
import math

import jax
import jax.numpy as jnp
import numpy as np
from jax import lax
from jax.experimental import pallas as pl
from jax.experimental.pallas import tpu as pltpu
from jax.sharding import PartitionSpec as P


HD = 128
ROWS = 512
LATC = 64
TILE = 16
TILES = ROWS // TILE
FAR = 24
REACH = FAR * TILE
SPAN = 2 * ROWS + 128
ACCR = 72
CHUNKS = (72, 58)
masked_score = -1e30
score_scale = math.log2(math.e) / math.sqrt(HD)
rope_theta = 10000.0
MESH = pl.DeviceIdType.MESH
SMEM = pl.BlockSpec(memory_space=pltpu.SMEM)
VMEM = pl.BlockSpec(memory_space=pltpu.VMEM)
ANY = pl.BlockSpec(memory_space=pl.ANY)


def share_static(ta, tb, heads):
    if ta > FAR:
        return 0
    if tb > FAR:
        return heads
    costs = [max(n * ta, (heads - n) * tb) for n in range(heads + 1)]
    return costs.index(min(costs))


def capacity(heads):
    most = 0
    for ta in range(1, TILES + 1):
        for tb in range(1, TILES + 2 - ta):
            n = share_static(ta, tb, heads)
            most = max(most, n * ta, (heads - n) * tb)
    return most


def chunk_tiles(heads):
    cap = capacity(heads)
    if cap >= 150:
        return CHUNKS + (cap - sum(CHUNKS),)
    return (FAR, cap - FAR)


def share(ta, tb, heads):
    best = heads * tb
    chosen = jnp.int32(0)
    for n in range(1, heads + 1):
        cost = jnp.maximum(n * ta, (heads - n) * tb)
        better = cost < best
        best = jnp.where(better, cost, best)
        chosen = jnp.where(better, n, chosen)
    chosen = jnp.where(tb > FAR, heads, chosen)
    return jnp.where(ta > FAR, 0, chosen)


def selector():
    pair_total = HD // 2
    side = HD // 6
    time = pair_total - 2 * side
    axis = np.array([0] * time + [1] * side + [2] * side)
    local = np.array(list(range(time)) + list(range(side)) * 2, np.float32)
    pairs = np.array([time] * time + [side] * (2 * side), np.float32)
    frequency = np.exp(-(local / pairs) * np.float32(math.log(rope_theta))).astype(np.float32)
    table = np.zeros((4, TILE, HD), np.float32)
    for group in range(4):
        for lane in range(HD):
            table[group, axis[lane // 2] * 4 + group, lane] = frequency[lane // 2]
    parts = []
    rest = table
    for _ in range(3):
        part = rest.astype(jnp.bfloat16)
        parts.append(part)
        rest = rest - part.astype(np.float32)
    return np.stack(parts)


def turner():
    table = np.zeros((2 * HD, 2 * HD), np.float32)
    for pair in range(HD):
        table[2 * pair + 1, 2 * pair] = -1.0
        table[2 * pair, 2 * pair + 1] = 1.0
    return table.astype(jnp.bfloat16)


def cdiv(value, unit):
    return (value + unit - 1) // unit


def pack_kernel(heads, chunks, lens_ref, pos_ref, q_ref, k_ref, v_ref, scal_ref, place_ref, *rest):
    count = len(chunks)
    right_refs, left_refs = rest[:count], rest[count : 2 * count]
    rows_in, packed, in_sem, out_sem = rest[2 * count :]
    groups = 4 if heads % 4 == 0 else 1
    width = heads // groups * HD
    loads = []
    for group in range(groups):
        columns = pl.ds(group * width, width)
        for j, source in enumerate((q_ref, k_ref, v_ref)):
            copy = pltpu.make_async_copy(
                source.at[:, :, columns],
                rows_in.at[j, pl.ds(0, TILES), :, columns],
                in_sem.at[group, j],
            )
            copy.start()
            loads.append(copy)
    low = lax.axis_index("req") * ROWS
    high = low + ROWS

    def scan(i, carry):
        end, start_low, end_low, start_high, end_high = carry
        start = end
        end = start + lens_ref[i]
        before_low = start < low
        before_high = start < high
        return (
            end,
            jnp.where(before_low, start, start_low),
            jnp.where(before_low, end, end_low),
            jnp.where(before_high, start, start_high),
            jnp.where(before_high, end, end_high),
        )

    zero = jnp.int32(0)
    _, start_low, end_low, start_high, end_high = lax.fori_loop(
        0, lens_ref.shape[0], scan, (zero, low, low, high, high), unroll=8
    )
    cut_low = end_low > low
    cut_high = end_high > high
    a_low = jnp.where(cut_low, low - start_low, 0)
    b_low = jnp.where(cut_low, end_low - low, 0)
    a_high = jnp.where(cut_high, high - start_high, 0)
    b_high = jnp.where(cut_high, end_high - high, 0)
    n_low = share(cdiv(a_low, TILE), cdiv(b_low, TILE), heads)
    n_high = share(cdiv(a_high, TILE), cdiv(b_high, TILE), heads)
    for i, value in enumerate((a_low, b_low, n_low, a_high, b_high, n_high)):
        scal_ref[i] = value
    scal_ref[6] = zero
    scal_ref[7] = zero

    placed = pos_ref[...].astype(jnp.float32)
    pieces = [placed[a : a + 1, g * HD : (g + 1) * HD] for a in range(3) for g in range(4)]
    pieces.append(jnp.zeros((TILE - 12, HD), jnp.float32))
    place_ref[...] = jnp.concatenate(pieces, axis=0).astype(jnp.bfloat16)
    for copy in loads:
        copy.wait()

    def pack(direction, first_tile, first_head, tiles, total):
        def one(slot, carry):
            columns = pl.ds(pl.multiple_of((first_head + slot) * HD, HD), HD)
            for j in range(3):
                packed[direction, j, pl.ds(slot * tiles, FAR)] = rows_in[
                    j, pl.ds(first_tile, FAR), :, columns
                ]
            return carry

        lax.fori_loop(0, total, one, 0)

    ta, tb = cdiv(a_high, TILE), cdiv(b_low, TILE)
    pack(0, TILES - ta, 0, ta, jnp.where(a_high > 0, n_high, 0))
    pack(1, 0, n_low, tb, jnp.where(b_low > 0, heads - n_low, 0))
    stores = []
    for direction, targets in enumerate((right_refs, left_refs)):
        begin = 0
        for c, tiles in enumerate(chunks):
            copy = pltpu.make_async_copy(
                packed.at[direction, :, pl.ds(begin, tiles)],
                targets[c].at[:, pl.ds(0, tiles)],
                out_sem.at[direction, c],
            )
            copy.start()
            stores.append(copy)
            begin += tiles
        copy = pltpu.make_async_copy(
            place_ref, targets[0].at[0, chunks[0]], out_sem.at[direction, count]
        )
        copy.start()
        stores.append(copy)
    for copy in stores:
        copy.wait()


def tables(place, select_ref, groups):
    parts = []
    for group in groups:
        angle = None
        for part in range(3):
            term = lax.dot_general(
                place,
                select_ref[part, group],
                (((0,), (0,)), ((), ())),
                preferred_element_type=jnp.float32,
            )
            angle = term if angle is None else angle + term
        parts.append(angle)
    angle = jnp.concatenate(parts, axis=0)
    return jnp.cos(angle), jnp.sin(angle)


def rotate(q, k, cosine, sine, turn):
    both = jnp.concatenate([q, k], axis=1)
    swapped = jnp.dot(both, turn, preferred_element_type=jnp.float32)
    return (
        q.astype(jnp.float32) * cosine + swapped[:, :HD] * sine,
        k.astype(jnp.float32) * cosine + swapped[:, HD:] * sine,
    )


def attend(q, k, v, bias):
    scores = lax.dot_general(k, q, (((1,), (1,)), ((), ())), preferred_element_type=jnp.float32)
    scores = scores + bias
    top = jnp.max(scores, axis=0, keepdims=True)
    weight = jnp.exp2((scores - top) * score_scale).astype(jnp.bfloat16)
    taller = jnp.concatenate([v.T, jnp.ones((TILE, v.shape[0]), jnp.bfloat16)], axis=0)
    summed = jnp.dot(taller, weight, preferred_element_type=jnp.float32)
    return (summed[:HD] * (1.0 / summed[HD : HD + 1])).astype(jnp.bfloat16)


def add_head(acc_ref, index, lanes, attended, w_block, scale_row):
    weights = (w_block.astype(jnp.float32) * (1.0 + scale_row)).astype(jnp.bfloat16)
    acc_ref[index + (pl.ds(0, LATC), lanes)] += jnp.dot(
        weights, attended, preferred_element_type=jnp.float32
    )
    wide = attended.astype(jnp.float32)
    squared = wide * wide
    total = squared[0:8]
    for part in range(1, HD // 8):
        total = total + squared[part * 8 : part * 8 + 8]
    acc_ref[index + (pl.ds(LATC, 8), lanes)] += total


def local_kernel(
    heads, lens_ref, step_ref, scal_ref, place_ref, select_ref, turn_ref, w_ref, mod_ref,
    q_ref, k_ref, v_ref, turned_ref, acc_ref, steps_ref, shift_ref,
    rows_in, cos_ref, sin_ref, bias_ref, mine, in_sem, out_sem,
):
    groups = 4 if heads % 4 == 0 else 1
    width = heads // groups * HD
    loads = []
    for group in range(groups):
        columns = pl.ds(group * width, width)
        for j, source in enumerate((q_ref, k_ref, v_ref)):
            copy = pltpu.make_async_copy(
                source.at[:, :, columns], rows_in.at[j, :, :, columns], in_sem.at[group, j]
            )
            copy.start()
            loads.append(copy)
    low = lax.axis_index("req") * ROWS
    lane = lax.broadcasted_iota(jnp.int32, (1, ROWS), 1) + low

    def label(i, carry):
        end, video, step = carry
        end = end + lens_ref[i]
        past = lane >= end
        video = video + past.astype(jnp.int32)
        following = step_ref[jnp.minimum(i + 1, lens_ref.shape[0] - 1)]
        return end, video, jnp.where(past, following, step)

    start = jnp.full((1, ROWS), step_ref[0], jnp.float32)
    _, video, step = lax.fori_loop(
        0, lens_ref.shape[0], label,
        (jnp.int32(0), jnp.zeros((1, ROWS), jnp.int32), start), unroll=8,
    )
    steps_ref[...] = step
    tall = jnp.broadcast_to(video.astype(jnp.float32), (HD, ROWS)).T
    for part in range(ROWS // HD):
        wide = jnp.broadcast_to(
            video[:, part * HD : (part + 1) * HD].astype(jnp.float32), (ROWS, HD)
        )
        bias_ref[:, part * HD : (part + 1) * HD] = jnp.where(tall == wide, 0.0, masked_score)
    cosine, sine = tables(place_ref[...], select_ref, range(4))
    cos_ref[...] = cosine
    sin_ref[...] = sine
    acc_ref[...] = jnp.zeros_like(acc_ref)
    shift = jnp.sum(w_ref[...].astype(jnp.float32) * mod_ref[0:1, :], axis=1, keepdims=True)
    shift_ref[...] = jnp.broadcast_to(shift, (LATC, HD))
    turn = turn_ref[...]
    for copy in loads:
        copy.wait()
    first = scal_ref[1]
    last = ROWS - scal_ref[3]
    begin = pl.multiple_of(first // HD * HD, HD)
    extent = jnp.where(first < last, cdiv(last, HD) * HD - begin, 0)

    def keep(head, slot):
        return pltpu.make_async_copy(mine.at[slot], turned_ref.at[head], out_sem.at[slot])

    def one(head, carry):
        slot = lax.rem(head, 2)
        columns = pl.ds(pl.multiple_of(head * HD, HD), HD)

        @pl.when(head >= 2)
        def _():
            keep(head, slot).wait()

        q = rows_in[0, :, :, columns].reshape(ROWS, HD)
        k = rows_in[1, :, :, columns].reshape(ROWS, HD)
        q, k = rotate(q, k, cos_ref[...], sin_ref[...], turn)
        mine[slot, 0] = q.astype(jnp.bfloat16)
        mine[slot, 1] = k.astype(jnp.bfloat16)
        mine[slot, 2] = rows_in[2, :, :, columns].reshape(ROWS, HD)
        keep(head, slot).start()
        for width in (128, 256, 384, 512):

            @pl.when(extent == width)
            def _(width=width):
                window = pl.ds(begin, width)
                attended = attend(
                    mine[slot, 0, window], mine[slot, 1, window], mine[slot, 2, window],
                    bias_ref[window, window],
                )
                add_head(acc_ref, (), window, attended, w_ref[:, columns], mod_ref[1:2, columns])

        return carry

    lax.fori_loop(0, heads, one, 0)
    for slot in range(2):
        keep(slot, slot).wait()


def cut_kernel(heads, chunks, c, *refs):
    final = c == len(chunks) - 1
    refs = list(refs)
    scal_ref, select_ref, turn_ref, w_ref, mod_ref, turned_ref = refs[:6]
    del refs[:6]
    here = [i for i in (c - 1, c) if i >= 0]
    sources = [refs[: len(here)], refs[len(here) : 2 * len(here)]]
    del refs[: 2 * len(here)]
    if c == 0:
        acc_ref, table_ref = refs[:2]
        del refs[:2]
    else:
        table_ref, before_ref = refs[:2]
        del refs[:2]
        if final:
            local_ref, own_ref, left_out, right_out = refs[:4]
            del refs[:4]
        else:
            acc_ref = refs.pop(0)
    if final:
        span, mine, recv, bias_ref, loc_sem, recv_sem, acc_ref = refs
    else:
        span, mine, recv, bias_ref, loc_sem, recv_sem = refs
    begins = [sum(chunks[:i]) for i in range(len(chunks) + 1)]
    base = begins[here[0]]
    loads = []
    for side in range(2):
        for i, index in enumerate(here):
            copy = pltpu.make_async_copy(
                sources[side][i].at[:, pl.ds(0, chunks[index])],
                recv.at[side, :, pl.ds(FAR + begins[index] - base, chunks[index])],
                recv_sem.at[side, i],
            )
            copy.start()
            loads.append(copy)
    if c == 0:
        place_copies = []
        for side in range(2):
            copy = pltpu.make_async_copy(
                sources[side][0].at[0, chunks[0]], recv.at[side, 0, 0], recv_sem.at[side, 2]
            )
            copy.start()
            place_copies.append(copy)
    a_low, b_low, n_low = scal_ref[0], scal_ref[1], scal_ref[2]
    a_high, b_high, n_high = scal_ref[3], scal_ref[4], scal_ref[5]
    ta_low, tb_low = cdiv(a_low, TILE), cdiv(b_low, TILE)
    ta_high, tb_high = cdiv(a_high, TILE), cdiv(b_high, TILE)

    def done(limit, tiles, total):
        if limit == 0:
            return jnp.int32(0)
        return jnp.where(tiles > 0, jnp.minimum(total, limit // jnp.maximum(tiles, 1)), 0)

    low_first = done(begins[c], ta_low, n_low)
    low_count = done(begins[c + 1], ta_low, n_low) - low_first
    high_first = done(begins[c], tb_high, heads - n_high)
    high_count = done(begins[c + 1], tb_high, heads - n_high) - high_first
    items = low_count + high_count

    def slot_of(i):
        return jnp.where(i < low_count, low_first + i, high_first + i - low_count)

    def head_of(i):
        return jnp.where(i < low_count, low_first + i, n_high + high_first + i - low_count)

    def fetch(i, buffer):
        return pltpu.make_async_copy(turned_ref.at[head_of(i)], mine.at[buffer], loc_sem.at[buffer])

    @pl.when(items > 0)
    def _():
        fetch(jnp.int32(0), 0).start()

    span[...] = jnp.zeros_like(span)
    shapes = []
    for side, (a, b, ta, tb) in enumerate(
        ((a_low, b_low, ta_low, tb_low), (a_high, b_high, ta_high, tb_high))
    ):
        over = ta + tb > TILES
        skip = jnp.where(over, TILE, 0)
        row = lax.broadcasted_iota(jnp.int32, (ROWS, HD), 0)
        spot = row + skip
        dead = ta * TILE - a
        valid = (spot >= dead) & (spot < ta * TILE + b)
        valid = valid | (over & (row - (ROWS - TILE) >= dead))
        bias_ref[side] = jnp.where(valid, 0.0, masked_score)
        shapes.append((over, ROWS - ta * TILE + skip))
    if c == 0:
        acc_ref[...] = jnp.zeros_like(acc_ref)
        for side, copy in enumerate(place_copies):
            copy.wait()
            groups = range(1, 4) if side == 0 else range(3)
            cosine, sine = tables(recv[side, 0, 0], select_ref, groups)
            table_ref[side, 0] = cosine
            table_ref[side, 1] = sine
    else:
        acc_ref[...] = before_ref[...]
    for copy in loads:
        copy.wait()
    turn = turn_ref[...]

    def one(i, carry):
        buffer = lax.rem(i, 2)
        fetch(i, buffer).wait()

        @pl.when(i + 1 < items)
        def _():
            fetch(i + 1, 1 - buffer).start()

        side = (i >= low_count).astype(jnp.int32)
        is_low = side == 0
        slot = slot_of(i)
        head = head_of(i)
        a = jnp.where(is_low, a_low, a_high)
        b = jnp.where(is_low, b_low, b_high)
        ta, tb = cdiv(a, TILE), cdiv(b, TILE)
        offset = jnp.where(is_low, slot * ta + ta, slot * tb + FAR) - base
        row = lax.broadcasted_iota(jnp.int32, (REACH, HD), 0)
        keep = (row >= jnp.where(is_low, REACH - ta * TILE, 0)) & (
            row < jnp.where(is_low, REACH, tb * TILE)
        )
        target = pl.ds(pl.multiple_of(jnp.where(is_low, ROWS - REACH, ROWS), 128), REACH)
        q, k, v = (recv[side, j, pl.ds(offset, FAR)].reshape(REACH, HD) for j in range(3))
        q, k = rotate(q, k, table_ref[side, 0], table_ref[side, 1], turn)
        for j, x in enumerate((q, k, v.astype(jnp.float32))):
            span[j, target] = jnp.where(keep, x, 0.0).astype(jnp.bfloat16)
        for j in range(3):
            span[j, pl.ds(pl.multiple_of(jnp.where(is_low, ROWS, 0), ROWS), ROWS)] = mine[buffer, j]
        over = ta + tb > TILES

        @pl.when(over)
        def _():
            ahead = pl.ds(pl.multiple_of(ROWS - ta * TILE, TILE), TILE)
            behind = pl.ds(pl.multiple_of(ROWS + (tb - 1) * TILE, TILE), TILE)
            mixed = lax.broadcasted_iota(jnp.int32, (TILE, HD), 0) < b - (tb - 1) * TILE
            for j in range(3):
                merged = jnp.where(
                    mixed, span[j, behind].astype(jnp.float32), span[j, ahead].astype(jnp.float32)
                )
                span[j, behind] = merged.astype(jnp.bfloat16)

        columns = pl.ds(pl.multiple_of(head * HD, HD), HD)
        start = pl.multiple_of(ROWS - ta * TILE + jnp.where(over, TILE, 0), TILE)
        extent = jnp.minimum(ta + tb, TILES) * TILE
        below = 0
        for width in (128, 256, 384, 512):

            @pl.when((extent > below) & (extent <= width))
            def _(width=width):
                rows = pl.ds(start, width)
                bias = jnp.concatenate([bias_ref[side, 0:width]] * (width // HD), axis=1)
                attended = attend(span[0, rows], span[1, rows], span[2, rows], bias)
                add_head(
                    acc_ref, (side,), pl.ds(0, width), attended,
                    w_ref[:, columns], mod_ref[1:2, columns],
                )

            below = width
        return carry

    lax.fori_loop(0, items, one, 0)
    if final:
        halves = []
        lane = lax.broadcasted_iota(jnp.int32, (ACCR, 2 * ROWS), 1)
        for side, (over, start) in enumerate(shapes):
            placed = jnp.concatenate([acc_ref[side], jnp.zeros((ACCR, ROWS), jnp.float32)], axis=1)
            placed = pltpu.roll(placed, start, 1)
            swapped = jnp.concatenate([placed[:, ROWS:], placed[:, :ROWS]], axis=1)
            extra = over & (lane < start)
            placed = jnp.where(extra, swapped, placed)
            halves.append((placed[:, :ROWS], placed[:, ROWS:]))
        lane = lax.broadcasted_iota(jnp.int32, (ACCR, ROWS), 1)
        own = jnp.where(lane < b_low, halves[0][1], 0.0)
        own = own + jnp.where(lane >= ROWS - a_high, halves[1][0], 0.0)
        own_ref[...] = own + jnp.where((lane >= b_low) & (lane < ROWS - a_high), local_ref[...], 0.0)
        back = jnp.where(lane >= ROWS - a_low, halves[0][0], 0.0)
        left_out[...] = back[:, ROWS - REACH :]
        back = jnp.where(lane < b_high, halves[1][1], 0.0)
        right_out[...] = back[:, :REACH]


def finish_kernel(
    features, ring, own_ref, left_ref, right_ref, shift_ref, guide_ref, out_ref,
    from_left, from_right, velocity, other, send_sem, recv_sem,
):
    me = lax.axis_index("req")
    parity = lax.axis_index("cfg")
    left, right = lax.rem(me + ring - 1, ring), lax.rem(me + 1, ring)
    partner = {"cfg": 1 - parity}
    barrier = pltpu.get_barrier_semaphore()
    for target in ({"req": left}, {"req": right}, partner):
        pl.semaphore_signal(barrier, inc=1, device_id=target, device_id_type=MESH)
    pl.semaphore_wait(barrier, 3)
    to_left = pltpu.make_async_remote_copy(
        left_ref, from_right, send_sem.at[0], recv_sem.at[0],
        device_id={"req": left}, device_id_type=MESH,
    )
    to_left.start()
    to_right = pltpu.make_async_remote_copy(
        right_ref, from_left, send_sem.at[1], recv_sem.at[1],
        device_id={"req": right}, device_id_type=MESH,
    )
    to_right.start()
    to_left.wait()
    to_right.wait()
    none = jnp.zeros((ACCR, ROWS - REACH), jnp.float32)
    total = own_ref[...]
    total = total + jnp.concatenate([none, from_right[...]], axis=1)
    total = total + jnp.concatenate([from_left[...], none], axis=1)
    square = jnp.sum(total[LATC:], axis=0, keepdims=True)
    inverse = lax.rsqrt(square * (1.0 / features) + 1e-06)
    velocity[...] = total[:LATC] * inverse + shift_ref[:, 0:1]
    half = LATC // 2
    give = pltpu.make_async_remote_copy(
        velocity.at[pl.ds(pl.multiple_of((1 - parity) * half, half), half)],
        other, send_sem.at[2], recv_sem.at[2], device_id=partner, device_id_type=MESH,
    )
    give.start()
    kept = velocity[pl.ds(pl.multiple_of(parity * half, half), half)]
    give.wait()
    theirs = other[...]
    conditional = jnp.where(parity == 0, kept, theirs)
    unconditional = jnp.where(parity == 0, theirs, kept)
    out_ref[...] = unconditional + guide_ref[0] * (conditional - unconditional)


def moved(value, step, ring):
    return lax.ppermute(value, "req", [(i, (i + step) % ring) for i in range(ring)])


def per_device(
    query_rows, key_rows, value_rows, positions, latents, w_head, modulation, guide_scale,
    step_sizes, lengths,
):
    features = query_rows.shape[2]
    heads = features // HD
    ring = lax.axis_size("req")
    chunks = chunk_tiles(heads)
    count = len(chunks)
    bf16, f32 = jnp.bfloat16, jnp.float32
    sized = jax.ShapeDtypeStruct
    q, k, v = query_rows[0], key_rows[0], value_rows[0]

    def tiled(x):
        return x.reshape(TILES, TILE, features)

    shapes = [sized((3, t + (i == 0), TILE, HD), bf16) for i, t in enumerate(chunks)]
    packed_tiles = sum(chunks) + FAR
    outs = pl.pallas_call(
        functools.partial(pack_kernel, heads, chunks),
        out_shape=[sized((8,), jnp.int32), sized((TILE, HD), bf16)] + shapes + shapes,
        in_specs=[SMEM, VMEM, ANY, ANY, ANY],
        out_specs=[SMEM, VMEM] + [ANY] * (2 * count),
        scratch_shapes=[
            pltpu.VMEM((3, TILES + FAR, TILE, features), bf16),
            pltpu.VMEM((2, 3, packed_tiles, TILE, HD), bf16),
            pltpu.SemaphoreType.DMA((4, 3)),
            pltpu.SemaphoreType.DMA((2, count + 1)),
        ],
        name="pack",
    )(lengths, positions, tiled(q), tiled(k), tiled(v))
    scal, place = outs[:2]
    to_right, to_left = outs[2 : 2 + count], outs[2 + count :]
    from_left = []
    from_right = []
    for c in range(count):
        from_left.append(moved(to_right[c], 1, ring))
        from_right.append(moved(to_left[c], -1, ring))

    select = jnp.asarray(selector())
    turn = jnp.asarray(turner())
    w_turned = w_head.T
    pair_ops = ROWS * ROWS * HD * 4
    turned, local_acc, steps, shift = pl.pallas_call(
        functools.partial(local_kernel, heads),
        out_shape=[
            sized((heads, 3, ROWS, HD), bf16),
            sized((ACCR, ROWS), f32),
            sized((1, ROWS), f32),
            sized((LATC, HD), f32),
        ],
        in_specs=[SMEM, SMEM, SMEM] + [VMEM] * 5 + [ANY] * 3,
        out_specs=[ANY, VMEM, VMEM, VMEM],
        scratch_shapes=[
            pltpu.VMEM((3, TILES, TILE, features), bf16),
            pltpu.VMEM((ROWS, HD), f32),
            pltpu.VMEM((ROWS, HD), f32),
            pltpu.VMEM((ROWS, ROWS), f32),
            pltpu.VMEM((2, 3, ROWS, HD), bf16),
            pltpu.SemaphoreType.DMA((4, 3)),
            pltpu.SemaphoreType.DMA((2,)),
        ],
        cost_estimate=pl.CostEstimate(
            flops=heads * pair_ops, bytes_accessed=6 * ROWS * features * 2, transcendentals=0
        ),
        name="local",
    )(
        lengths, step_sizes, scal, place, select, turn, w_turned, modulation,
        tiled(q), tiled(k), tiled(v),
    )

    acc = table = None
    for c in range(count):
        final = c == count - 1
        here = [i for i in (c - 1, c) if i >= 0]
        operands = [scal, select, turn, w_turned, modulation, turned]
        specs = [SMEM, VMEM, VMEM, VMEM, VMEM, ANY]
        operands += [from_left[i] for i in here] + [from_right[i] for i in here]
        specs += [ANY] * (2 * len(here))
        if c > 0:
            operands += [table, acc]
            specs += [VMEM, VMEM]
        acc_shape = sized((2, ACCR, ROWS), f32)
        if final:
            operands.append(local_acc)
            specs.append(VMEM)
            out_shape = [
                sized((ACCR, ROWS), f32),
                sized((ACCR, REACH), f32),
                sized((ACCR, REACH), f32),
            ]
        elif c == 0:
            out_shape = [acc_shape, sized((2, 2, REACH, HD), f32)]
        else:
            out_shape = [acc_shape]
        scratch = [
            pltpu.VMEM((3, SPAN, HD), bf16),
            pltpu.VMEM((2, 3, ROWS, HD), bf16),
            pltpu.VMEM((2, 3, 2 * FAR + sum(chunks[i] for i in here), TILE, HD), bf16),
            pltpu.VMEM((2, ROWS, HD), f32),
            pltpu.SemaphoreType.DMA((2,)),
            pltpu.SemaphoreType.DMA((2, 3)),
        ]
        if final:
            scratch.append(pltpu.VMEM((2, ACCR, ROWS), f32))
        results = pl.pallas_call(
            functools.partial(cut_kernel, heads, chunks, c),
            out_shape=out_shape,
            in_specs=specs,
            out_specs=[VMEM] * len(out_shape),
            scratch_shapes=scratch,
            cost_estimate=pl.CostEstimate(
                flops=heads * pair_ops // count, bytes_accessed=4 << 20, transcendentals=0
            ),
        )(*operands)
        if final:
            own, back_left, back_right = results
        elif c == 0:
            acc, table = results
        else:
            (acc,) = results

    guided = pl.pallas_call(
        functools.partial(finish_kernel, features, ring),
        out_shape=sized((LATC // 2, ROWS), f32),
        in_specs=[VMEM, VMEM, VMEM, VMEM, SMEM],
        out_specs=VMEM,
        scratch_shapes=[
            pltpu.VMEM((ACCR, REACH), f32),
            pltpu.VMEM((ACCR, REACH), f32),
            pltpu.VMEM((LATC, ROWS), f32),
            pltpu.VMEM((LATC // 2, ROWS), f32),
            pltpu.SemaphoreType.DMA((3,)),
            pltpu.SemaphoreType.DMA((3,)),
        ],
        compiler_params=pltpu.CompilerParams(collective_id=0, has_side_effects=True),
        name="finish",
    )(own, back_left, back_right, shift, guide_scale)
    return (latents.T + steps * guided).T


def solution(mesh):
    in_specs = (
        P("cfg", "req", None),
        P("cfg", "req", None),
        P("cfg", "req", None),
        P(None, "req"),
        P("req", "cfg"),
        P(),
        P(),
        P(),
        P(),
        P(),
    )
    return jax.shard_map(
        per_device, mesh=mesh, in_specs=in_specs, out_specs=P("req", "cfg"), check_vma=False
    )
```

```python
import functools
import math

import jax
import jax.numpy as jnp
import numpy as np
from jax import lax
from jax.experimental import pallas as pl
from jax.experimental.pallas import tpu as pltpu
from jax.sharding import PartitionSpec as P


HD = 128
ROWS = 512
LATC = 64
TILE = 16
TILES = ROWS // TILE
FAR = 24
REACH = FAR * TILE
SPAN = 2 * ROWS + 128
ACCR = 72
CHUNKS = (104,)
masked_score = -1e30
score_scale = math.log2(math.e) / math.sqrt(HD)
rope_theta = 10000.0
MESH = pl.DeviceIdType.MESH
SMEM = pl.BlockSpec(memory_space=pltpu.SMEM)
VMEM = pl.BlockSpec(memory_space=pltpu.VMEM)
ANY = pl.BlockSpec(memory_space=pl.ANY)


def share_static(ta, tb, heads):
    if ta > FAR:
        return 0
    if tb > FAR:
        return heads
    costs = [max(n * ta, (heads - n) * tb) for n in range(heads + 1)]
    return costs.index(min(costs))


def capacity(heads):
    most = 0
    for ta in range(1, TILES + 1):
        for tb in range(1, TILES + 2 - ta):
            n = share_static(ta, tb, heads)
            most = max(most, n * ta, (heads - n) * tb)
    return most


def chunk_tiles(heads):
    cap = capacity(heads)
    if cap >= 150:
        return CHUNKS + (cap - sum(CHUNKS),)
    return (FAR, cap - FAR)


def share(ta, tb, heads):
    best = heads * tb
    chosen = jnp.int32(0)
    for n in range(1, heads + 1):
        cost = jnp.maximum(n * ta, (heads - n) * tb)
        better = cost < best
        best = jnp.where(better, cost, best)
        chosen = jnp.where(better, n, chosen)
    chosen = jnp.where(tb > FAR, heads, chosen)
    return jnp.where(ta > FAR, 0, chosen)


def selector():
    pair_total = HD // 2
    side = HD // 6
    time = pair_total - 2 * side
    axis = np.array([0] * time + [1] * side + [2] * side)
    local = np.array(list(range(time)) + list(range(side)) * 2, np.float32)
    pairs = np.array([time] * time + [side] * (2 * side), np.float32)
    frequency = np.exp(-(local / pairs) * np.float32(math.log(rope_theta))).astype(np.float32)
    table = np.zeros((4, TILE, HD), np.float32)
    for group in range(4):
        for lane in range(HD):
            table[group, axis[lane // 2] * 4 + group, lane] = frequency[lane // 2]
    parts = []
    rest = table
    for _ in range(3):
        part = rest.astype(jnp.bfloat16)
        parts.append(part)
        rest = rest - part.astype(np.float32)
    return np.stack(parts)


def turner():
    table = np.zeros((2 * HD, 2 * HD), np.float32)
    for pair in range(HD):
        table[2 * pair + 1, 2 * pair] = -1.0
        table[2 * pair, 2 * pair + 1] = 1.0
    return table.astype(jnp.bfloat16)


def cdiv(value, unit):
    return (value + unit - 1) // unit


def pack_kernel(heads, chunks, lens_ref, pos_ref, q_ref, k_ref, v_ref, scal_ref, place_ref, *rest):
    count = len(chunks)
    right_refs, left_refs = rest[:count], rest[count : 2 * count]
    rows_in, packed, in_sem, out_sem = rest[2 * count :]
    groups = 4 if heads % 4 == 0 else 1
    width = heads // groups * HD
    loads = []
    for group in range(groups):
        columns = pl.ds(group * width, width)
        for j, source in enumerate((q_ref, k_ref, v_ref)):
            copy = pltpu.make_async_copy(
                source.at[:, :, columns],
                rows_in.at[j, pl.ds(0, TILES), :, columns],
                in_sem.at[group, j],
            )
            copy.start()
            loads.append(copy)
    low = lax.axis_index("req") * ROWS
    high = low + ROWS

    def scan(i, carry):
        end, start_low, end_low, start_high, end_high = carry
        start = end
        end = start + lens_ref[i]
        before_low = start < low
        before_high = start < high
        return (
            end,
            jnp.where(before_low, start, start_low),
            jnp.where(before_low, end, end_low),
            jnp.where(before_high, start, start_high),
            jnp.where(before_high, end, end_high),
        )

    zero = jnp.int32(0)
    _, start_low, end_low, start_high, end_high = lax.fori_loop(
        0, lens_ref.shape[0], scan, (zero, low, low, high, high), unroll=8
    )
    cut_low = end_low > low
    cut_high = end_high > high
    a_low = jnp.where(cut_low, low - start_low, 0)
    b_low = jnp.where(cut_low, end_low - low, 0)
    a_high = jnp.where(cut_high, high - start_high, 0)
    b_high = jnp.where(cut_high, end_high - high, 0)
    n_low = share(cdiv(a_low, TILE), cdiv(b_low, TILE), heads)
    n_high = share(cdiv(a_high, TILE), cdiv(b_high, TILE), heads)
    for i, value in enumerate((a_low, b_low, n_low, a_high, b_high, n_high)):
        scal_ref[i] = value
    scal_ref[6] = zero
    scal_ref[7] = zero

    placed = pos_ref[...].astype(jnp.float32)
    pieces = [placed[a : a + 1, g * HD : (g + 1) * HD] for a in range(3) for g in range(4)]
    pieces.append(jnp.zeros((TILE - 12, HD), jnp.float32))
    place_ref[...] = jnp.concatenate(pieces, axis=0).astype(jnp.bfloat16)

    def pack(direction, first_tile, first_head, tiles, begin, end):
        def one(head, carry):
            columns = pl.ds(pl.multiple_of(head * HD, HD), HD)
            for j in range(3):
                packed[direction, j, pl.ds((head - first_head) * tiles, FAR)] = rows_in[
                    j, pl.ds(first_tile, FAR), :, columns
                ]
            return carry

        lax.fori_loop(begin, end, one, 0)

    ta, tb = cdiv(a_high, TILE), cdiv(b_low, TILE)
    last_right = jnp.where(a_high > 0, n_high, 0)
    first_left = jnp.where(b_low > 0, n_low, heads)
    each = heads // groups
    for group in range(groups):
        for copy in loads[3 * group : 3 * group + 3]:
            copy.wait()
        begin, end = group * each, (group + 1) * each
        pack(0, TILES - ta, 0, ta, begin, jnp.minimum(end, last_right))
        pack(1, 0, n_low, tb, jnp.maximum(begin, first_left), end)
    stores = []
    for direction, targets in enumerate((right_refs, left_refs)):
        begin = 0
        for c, tiles in enumerate(chunks):
            copy = pltpu.make_async_copy(
                packed.at[direction, :, pl.ds(begin, tiles)],
                targets[c].at[:, pl.ds(0, tiles)],
                out_sem.at[direction, c],
            )
            copy.start()
            stores.append(copy)
            begin += tiles
        copy = pltpu.make_async_copy(
            place_ref, targets[0].at[0, chunks[0]], out_sem.at[direction, count]
        )
        copy.start()
        stores.append(copy)
    for copy in stores:
        copy.wait()


def tables(place, select_ref, groups):
    parts = []
    for group in groups:
        angle = None
        for part in range(3):
            term = lax.dot_general(
                place,
                select_ref[part, group],
                (((0,), (0,)), ((), ())),
                preferred_element_type=jnp.float32,
            )
            angle = term if angle is None else angle + term
        parts.append(angle)
    angle = jnp.concatenate(parts, axis=0)
    return jnp.cos(angle), jnp.sin(angle)


def rotate(q, k, cosine, sine, turn):
    both = jnp.concatenate([q, k], axis=1)
    swapped = jnp.dot(both, turn, preferred_element_type=jnp.float32)
    return (
        q.astype(jnp.float32) * cosine + swapped[:, :HD] * sine,
        k.astype(jnp.float32) * cosine + swapped[:, HD:] * sine,
    )


def attend(q, k, v, bias):
    scores = lax.dot_general(k, q, (((1,), (1,)), ((), ())), preferred_element_type=jnp.float32)
    scores = scores + bias
    top = jnp.max(scores, axis=0, keepdims=True)
    weight = jnp.exp2((scores - top) * score_scale).astype(jnp.bfloat16)
    taller = jnp.concatenate([v.T, jnp.ones((TILE, v.shape[0]), jnp.bfloat16)], axis=0)
    summed = jnp.dot(taller, weight, preferred_element_type=jnp.float32)
    return (summed[:HD] * (1.0 / summed[HD : HD + 1])).astype(jnp.bfloat16)


def add_head(acc_ref, index, lanes, attended, w_block, scale_row):
    weights = (w_block.astype(jnp.float32) * (1.0 + scale_row)).astype(jnp.bfloat16)
    acc_ref[index + (pl.ds(0, LATC), lanes)] += jnp.dot(
        weights, attended, preferred_element_type=jnp.float32
    )
    wide = attended.astype(jnp.float32)
    squared = wide * wide
    total = squared[0:8]
    for part in range(1, HD // 8):
        total = total + squared[part * 8 : part * 8 + 8]
    acc_ref[index + (pl.ds(LATC, 8), lanes)] += total


def local_kernel(
    heads, lens_ref, step_ref, scal_ref, place_ref, select_ref, turn_ref, w_ref, mod_ref,
    q_ref, k_ref, v_ref, turned_ref, acc_ref, steps_ref, shift_ref,
    rows_in, cos_ref, sin_ref, bias_ref, mine, in_sem, out_sem,
):
    groups = 4 if heads % 4 == 0 else 1
    width = heads // groups * HD
    loads = []
    for group in range(groups):
        columns = pl.ds(group * width, width)
        for j, source in enumerate((q_ref, k_ref, v_ref)):
            copy = pltpu.make_async_copy(
                source.at[:, :, columns], rows_in.at[j, :, :, columns], in_sem.at[group, j]
            )
            copy.start()
            loads.append(copy)
    low = lax.axis_index("req") * ROWS
    lane = lax.broadcasted_iota(jnp.int32, (1, ROWS), 1) + low

    def label(i, carry):
        end, video, step = carry
        end = end + lens_ref[i]
        past = lane >= end
        video = video + past.astype(jnp.int32)
        following = step_ref[jnp.minimum(i + 1, lens_ref.shape[0] - 1)]
        return end, video, jnp.where(past, following, step)

    start = jnp.full((1, ROWS), step_ref[0], jnp.float32)
    _, video, step = lax.fori_loop(
        0, lens_ref.shape[0], label,
        (jnp.int32(0), jnp.zeros((1, ROWS), jnp.int32), start), unroll=8,
    )
    steps_ref[...] = step
    tall = jnp.broadcast_to(video.astype(jnp.float32), (HD, ROWS)).T
    for part in range(ROWS // HD):
        wide = jnp.broadcast_to(
            video[:, part * HD : (part + 1) * HD].astype(jnp.float32), (ROWS, HD)
        )
        bias_ref[:, part * HD : (part + 1) * HD] = jnp.where(tall == wide, 0.0, masked_score)
    cosine, sine = tables(place_ref[...], select_ref, range(4))
    cos_ref[...] = cosine
    sin_ref[...] = sine
    acc_ref[...] = jnp.zeros_like(acc_ref)
    shift = jnp.sum(w_ref[...].astype(jnp.float32) * mod_ref[0:1, :], axis=1, keepdims=True)
    shift_ref[...] = jnp.broadcast_to(shift, (LATC, HD))
    turn = turn_ref[...]
    for copy in loads:
        copy.wait()
    first = scal_ref[1]
    last = ROWS - scal_ref[3]
    begin = pl.multiple_of(first // HD * HD, HD)
    extent = jnp.where(first < last, cdiv(last, HD) * HD - begin, 0)

    def keep(head, slot):
        return pltpu.make_async_copy(mine.at[slot], turned_ref.at[head], out_sem.at[slot])

    def one(head, carry):
        slot = lax.rem(head, 2)
        columns = pl.ds(pl.multiple_of(head * HD, HD), HD)

        @pl.when(head >= 2)
        def _():
            keep(head, slot).wait()

        q = rows_in[0, :, :, columns].reshape(ROWS, HD)
        k = rows_in[1, :, :, columns].reshape(ROWS, HD)
        q, k = rotate(q, k, cos_ref[...], sin_ref[...], turn)
        mine[slot, 0] = q.astype(jnp.bfloat16)
        mine[slot, 1] = k.astype(jnp.bfloat16)
        mine[slot, 2] = rows_in[2, :, :, columns].reshape(ROWS, HD)
        keep(head, slot).start()
        for width in (128, 256, 384, 512):

            @pl.when(extent == width)
            def _(width=width):
                window = pl.ds(begin, width)
                attended = attend(
                    mine[slot, 0, window], mine[slot, 1, window], mine[slot, 2, window],
                    bias_ref[window, window],
                )
                add_head(acc_ref, (), window, attended, w_ref[:, columns], mod_ref[1:2, columns])

        return carry

    lax.fori_loop(0, heads, one, 0)
    for slot in range(2):
        keep(slot, slot).wait()


def cut_kernel(heads, chunks, c, *refs):
    final = c == len(chunks) - 1
    refs = list(refs)
    scal_ref, select_ref, turn_ref, w_ref, mod_ref, turned_ref = refs[:6]
    del refs[:6]
    here = [i for i in (c - 1, c) if i >= 0]
    sources = [refs[: len(here)], refs[len(here) : 2 * len(here)]]
    del refs[: 2 * len(here)]
    if c == 0:
        acc_ref, table_ref = refs[:2]
        del refs[:2]
    else:
        table_ref, before_ref = refs[:2]
        del refs[:2]
        if final:
            local_ref, own_ref, left_out, right_out = refs[:4]
            del refs[:4]
        else:
            acc_ref = refs.pop(0)
    if final:
        span, recv, bias_ref, loc_sem, recv_sem, acc_ref = refs
    else:
        span, recv, bias_ref, loc_sem, recv_sem = refs
    begins = [sum(chunks[:i]) for i in range(len(chunks) + 1)]
    base = begins[here[0]]
    loads = []
    for side in range(2):
        for i, index in enumerate(here):
            copy = pltpu.make_async_copy(
                sources[side][i].at[:, pl.ds(0, chunks[index])],
                recv.at[side, :, pl.ds(FAR + begins[index] - base, chunks[index])],
                recv_sem.at[side, i],
            )
            copy.start()
            loads.append(copy)
    if c == 0:
        place_copies = []
        for side in range(2):
            copy = pltpu.make_async_copy(
                sources[side][0].at[0, chunks[0]], recv.at[side, 0, 0], recv_sem.at[side, 2]
            )
            copy.start()
            place_copies.append(copy)
    a_low, b_low, n_low = scal_ref[0], scal_ref[1], scal_ref[2]
    a_high, b_high, n_high = scal_ref[3], scal_ref[4], scal_ref[5]
    ta_low, tb_low = cdiv(a_low, TILE), cdiv(b_low, TILE)
    ta_high, tb_high = cdiv(a_high, TILE), cdiv(b_high, TILE)

    def done(limit, tiles, total):
        if limit == 0:
            return jnp.int32(0)
        return jnp.where(tiles > 0, jnp.minimum(total, limit // jnp.maximum(tiles, 1)), 0)

    low_first = done(begins[c], ta_low, n_low)
    low_count = done(begins[c + 1], ta_low, n_low) - low_first
    high_first = done(begins[c], tb_high, heads - n_high)
    high_count = done(begins[c + 1], tb_high, heads - n_high) - high_first
    items = low_count + high_count

    def slot_of(i):
        return jnp.where(i < low_count, low_first + i, high_first + i - low_count)

    def head_of(i):
        return jnp.where(i < low_count, low_first + i, n_high + high_first + i - low_count)

    def fetch(i, buffer):
        rows = pl.ds(pl.multiple_of(jnp.where(i < low_count, ROWS, 0), ROWS), ROWS)
        return pltpu.make_async_copy(
            turned_ref.at[head_of(i)], span.at[buffer, :, rows], loc_sem.at[buffer]
        )

    span[...] = jnp.zeros_like(span)
    shapes = []
    for side, (a, b, ta, tb) in enumerate(
        ((a_low, b_low, ta_low, tb_low), (a_high, b_high, ta_high, tb_high))
    ):
        over = ta + tb > TILES
        skip = jnp.where(over, TILE, 0)
        row = lax.broadcasted_iota(jnp.int32, (ROWS, HD), 0)
        spot = row + skip
        dead = ta * TILE - a
        valid = (spot >= dead) & (spot < ta * TILE + b)
        valid = valid | (over & (row - (ROWS - TILE) >= dead))
        bias_ref[side] = jnp.where(valid, 0.0, masked_score)
        shapes.append((over, ROWS - ta * TILE + skip))
    if c == 0:
        acc_ref[...] = jnp.zeros_like(acc_ref)
        for side, copy in enumerate(place_copies):
            copy.wait()
            groups = range(1, 4) if side == 0 else range(3)
            cosine, sine = tables(recv[side, 0, 0], select_ref, groups)
            table_ref[side, 0] = cosine
            table_ref[side, 1] = sine
    else:
        acc_ref[...] = before_ref[...]

    @pl.when(items > 0)
    def _():
        fetch(jnp.int32(0), 0).start()

    for copy in loads:
        copy.wait()
    turn = turn_ref[...]

    def one(i, carry):
        buffer = lax.rem(i, 2)
        fetch(i, buffer).wait()

        @pl.when(i + 1 < items)
        def _():
            fetch(i + 1, 1 - buffer).start()

        side = (i >= low_count).astype(jnp.int32)
        is_low = side == 0
        slot = slot_of(i)
        head = head_of(i)
        a = jnp.where(is_low, a_low, a_high)
        b = jnp.where(is_low, b_low, b_high)
        ta, tb = cdiv(a, TILE), cdiv(b, TILE)
        offset = jnp.where(is_low, slot * ta + ta, slot * tb + FAR) - base
        first = jnp.where(is_low, REACH - ta * TILE, 0)
        last = jnp.where(is_low, REACH, tb * TILE)
        target = jnp.where(is_low, ROWS - REACH, ROWS)
        for block in range(REACH // HD):
            low, high = block * HD, (block + 1) * HD

            @pl.when((first < high) & (last > low))
            def _(low=low, high=high):
                row = lax.broadcasted_iota(jnp.int32, (HD, HD), 0) + low
                keep = (row >= first) & (row < last)
                tiles = pl.ds(offset + low // TILE, HD // TILE)
                q, k, v = (recv[side, j, tiles].reshape(HD, HD) for j in range(3))
                cosine, sine = table_ref[side, 0, low:high], table_ref[side, 1, low:high]
                q, k = rotate(q, k, cosine, sine, turn)
                rows = pl.ds(pl.multiple_of(target + low, HD), HD)
                for j, x in enumerate((q, k, v.astype(jnp.float32))):
                    span[buffer, j, rows] = jnp.where(keep, x, 0.0).astype(jnp.bfloat16)

        over = ta + tb > TILES

        @pl.when(over)
        def _():
            ahead = pl.ds(pl.multiple_of(ROWS - ta * TILE, TILE), TILE)
            behind = pl.ds(pl.multiple_of(ROWS + (tb - 1) * TILE, TILE), TILE)
            mixed = lax.broadcasted_iota(jnp.int32, (TILE, HD), 0) < b - (tb - 1) * TILE
            for j in range(3):
                merged = jnp.where(
                    mixed, span[buffer, j, behind].astype(jnp.float32), span[buffer, j, ahead].astype(jnp.float32)
                )
                span[buffer, j, behind] = merged.astype(jnp.bfloat16)

        columns = pl.ds(pl.multiple_of(head * HD, HD), HD)
        start = pl.multiple_of(ROWS - ta * TILE + jnp.where(over, TILE, 0), TILE)
        extent = jnp.minimum(ta + tb, TILES) * TILE
        below = 0
        for width in (128, 256, 384, 512):

            @pl.when((extent > below) & (extent <= width))
            def _(width=width):
                rows = pl.ds(start, width)
                bias = jnp.concatenate([bias_ref[side, 0:width]] * (width // HD), axis=1)
                attended = attend(
                    span[buffer, 0, rows], span[buffer, 1, rows], span[buffer, 2, rows], bias
                )
                add_head(
                    acc_ref, (side,), pl.ds(0, width), attended,
                    w_ref[:, columns], mod_ref[1:2, columns],
                )

            below = width
        return carry

    lax.fori_loop(0, items, one, 0)
    if final:
        halves = []
        lane = lax.broadcasted_iota(jnp.int32, (ACCR, 2 * ROWS), 1)
        for side, (over, start) in enumerate(shapes):
            placed = jnp.concatenate([acc_ref[side], jnp.zeros((ACCR, ROWS), jnp.float32)], axis=1)
            placed = pltpu.roll(placed, start, 1)
            swapped = jnp.concatenate([placed[:, ROWS:], placed[:, :ROWS]], axis=1)
            extra = over & (lane < start)
            placed = jnp.where(extra, swapped, placed)
            halves.append((placed[:, :ROWS], placed[:, ROWS:]))
        lane = lax.broadcasted_iota(jnp.int32, (ACCR, ROWS), 1)
        own = jnp.where(lane < b_low, halves[0][1], 0.0)
        own = own + jnp.where(lane >= ROWS - a_high, halves[1][0], 0.0)
        own_ref[...] = own + jnp.where((lane >= b_low) & (lane < ROWS - a_high), local_ref[...], 0.0)
        back = jnp.where(lane >= ROWS - a_low, halves[0][0], 0.0)
        left_out[...] = back[:, ROWS - REACH :]
        back = jnp.where(lane < b_high, halves[1][1], 0.0)
        right_out[...] = back[:, :REACH]


def finish_kernel(
    features, ring, own_ref, left_ref, right_ref, shift_ref, guide_ref, out_ref,
    from_left, from_right, velocity, other, send_sem, recv_sem,
):
    me = lax.axis_index("req")
    parity = lax.axis_index("cfg")
    left, right = lax.rem(me + ring - 1, ring), lax.rem(me + 1, ring)
    partner = {"cfg": 1 - parity}
    barrier = pltpu.get_barrier_semaphore()
    for target in ({"req": left}, {"req": right}, partner):
        pl.semaphore_signal(barrier, inc=1, device_id=target, device_id_type=MESH)
    pl.semaphore_wait(barrier, 3)
    to_left = pltpu.make_async_remote_copy(
        left_ref, from_right, send_sem.at[0], recv_sem.at[0],
        device_id={"req": left}, device_id_type=MESH,
    )
    to_left.start()
    to_right = pltpu.make_async_remote_copy(
        right_ref, from_left, send_sem.at[1], recv_sem.at[1],
        device_id={"req": right}, device_id_type=MESH,
    )
    to_right.start()
    to_left.wait()
    to_right.wait()
    none = jnp.zeros((ACCR, ROWS - REACH), jnp.float32)
    total = own_ref[...]
    total = total + jnp.concatenate([none, from_right[...]], axis=1)
    total = total + jnp.concatenate([from_left[...], none], axis=1)
    square = jnp.sum(total[LATC:], axis=0, keepdims=True)
    inverse = lax.rsqrt(square * (1.0 / features) + 1e-06)
    velocity[...] = total[:LATC] * inverse + shift_ref[:, 0:1]
    half = LATC // 2
    give = pltpu.make_async_remote_copy(
        velocity.at[pl.ds(pl.multiple_of((1 - parity) * half, half), half)],
        other, send_sem.at[2], recv_sem.at[2], device_id=partner, device_id_type=MESH,
    )
    give.start()
    kept = velocity[pl.ds(pl.multiple_of(parity * half, half), half)]
    give.wait()
    theirs = other[...]
    conditional = jnp.where(parity == 0, kept, theirs)
    unconditional = jnp.where(parity == 0, theirs, kept)
    out_ref[...] = unconditional + guide_ref[0] * (conditional - unconditional)


def moved(value, step, ring):
    return lax.ppermute(value, "req", [(i, (i + step) % ring) for i in range(ring)])


def per_device(
    query_rows, key_rows, value_rows, positions, latents, w_head, modulation, guide_scale,
    step_sizes, lengths,
):
    features = query_rows.shape[2]
    heads = features // HD
    ring = lax.axis_size("req")
    chunks = chunk_tiles(heads)
    count = len(chunks)
    bf16, f32 = jnp.bfloat16, jnp.float32
    sized = jax.ShapeDtypeStruct
    q, k, v = query_rows[0], key_rows[0], value_rows[0]

    def tiled(x):
        return x.reshape(TILES, TILE, features)

    shapes = [sized((3, t + (i == 0), TILE, HD), bf16) for i, t in enumerate(chunks)]
    packed_tiles = sum(chunks) + FAR
    outs = pl.pallas_call(
        functools.partial(pack_kernel, heads, chunks),
        out_shape=[sized((8,), jnp.int32), sized((TILE, HD), bf16)] + shapes + shapes,
        in_specs=[SMEM, VMEM, ANY, ANY, ANY],
        out_specs=[SMEM, VMEM] + [ANY] * (2 * count),
        scratch_shapes=[
            pltpu.VMEM((3, TILES + FAR, TILE, features), bf16),
            pltpu.VMEM((2, 3, packed_tiles, TILE, HD), bf16),
            pltpu.SemaphoreType.DMA((4, 3)),
            pltpu.SemaphoreType.DMA((2, count + 1)),
        ],
        name="pack",
    )(lengths, positions, tiled(q), tiled(k), tiled(v))
    scal, place = outs[:2]
    to_right, to_left = outs[2 : 2 + count], outs[2 + count :]
    from_left = []
    from_right = []
    for c in range(count):
        from_left.append(moved(to_right[c], 1, ring))
        from_right.append(moved(to_left[c], -1, ring))

    select = jnp.asarray(selector())
    turn = jnp.asarray(turner())
    w_turned = w_head.T
    pair_ops = ROWS * ROWS * HD * 4
    turned, local_acc, steps, shift = pl.pallas_call(
        functools.partial(local_kernel, heads),
        out_shape=[
            sized((heads, 3, ROWS, HD), bf16),
            sized((ACCR, ROWS), f32),
            sized((1, ROWS), f32),
            sized((LATC, HD), f32),
        ],
        in_specs=[SMEM, SMEM, SMEM] + [VMEM] * 5 + [ANY] * 3,
        out_specs=[ANY, VMEM, VMEM, VMEM],
        scratch_shapes=[
            pltpu.VMEM((3, TILES, TILE, features), bf16),
            pltpu.VMEM((ROWS, HD), f32),
            pltpu.VMEM((ROWS, HD), f32),
            pltpu.VMEM((ROWS, ROWS), f32),
            pltpu.VMEM((2, 3, ROWS, HD), bf16),
            pltpu.SemaphoreType.DMA((4, 3)),
            pltpu.SemaphoreType.DMA((2,)),
        ],
        cost_estimate=pl.CostEstimate(
            flops=heads * pair_ops, bytes_accessed=6 * ROWS * features * 2, transcendentals=0
        ),
        name="local",
    )(
        lengths, step_sizes, scal, place, select, turn, w_turned, modulation,
        tiled(q), tiled(k), tiled(v),
    )

    acc = table = None
    for c in range(count):
        final = c == count - 1
        here = [i for i in (c - 1, c) if i >= 0]
        operands = [scal, select, turn, w_turned, modulation, turned]
        specs = [SMEM, VMEM, VMEM, VMEM, VMEM, ANY]
        operands += [from_left[i] for i in here] + [from_right[i] for i in here]
        specs += [ANY] * (2 * len(here))
        if c > 0:
            operands += [table, acc]
            specs += [VMEM, VMEM]
        acc_shape = sized((2, ACCR, ROWS), f32)
        if final:
            operands.append(local_acc)
            specs.append(VMEM)
            out_shape = [
                sized((ACCR, ROWS), f32),
                sized((ACCR, REACH), f32),
                sized((ACCR, REACH), f32),
            ]
        elif c == 0:
            out_shape = [acc_shape, sized((2, 2, REACH, HD), f32)]
        else:
            out_shape = [acc_shape]
        scratch = [
            pltpu.VMEM((2, 3, SPAN, HD), bf16),
            pltpu.VMEM((2, 3, 2 * FAR + sum(chunks[i] for i in here), TILE, HD), bf16),
            pltpu.VMEM((2, ROWS, HD), f32),
            pltpu.SemaphoreType.DMA((2,)),
            pltpu.SemaphoreType.DMA((2, 3)),
        ]
        if final:
            scratch.append(pltpu.VMEM((2, ACCR, ROWS), f32))
        results = pl.pallas_call(
            functools.partial(cut_kernel, heads, chunks, c),
            out_shape=out_shape,
            in_specs=specs,
            out_specs=[VMEM] * len(out_shape),
            scratch_shapes=scratch,
            cost_estimate=pl.CostEstimate(
                flops=heads * pair_ops // count, bytes_accessed=4 << 20, transcendentals=0
            ),
        )(*operands)
        if final:
            own, back_left, back_right = results
        elif c == 0:
            acc, table = results
        else:
            (acc,) = results

    guided = pl.pallas_call(
        functools.partial(finish_kernel, features, ring),
        out_shape=sized((LATC // 2, ROWS), f32),
        in_specs=[VMEM, VMEM, VMEM, VMEM, SMEM],
        out_specs=VMEM,
        scratch_shapes=[
            pltpu.VMEM((ACCR, REACH), f32),
            pltpu.VMEM((ACCR, REACH), f32),
            pltpu.VMEM((LATC, ROWS), f32),
            pltpu.VMEM((LATC // 2, ROWS), f32),
            pltpu.SemaphoreType.DMA((3,)),
            pltpu.SemaphoreType.DMA((3,)),
        ],
        compiler_params=pltpu.CompilerParams(collective_id=0, has_side_effects=True),
        name="finish",
    )(own, back_left, back_right, shift, guide_scale)
    return (latents.T + steps * guided).T


def solution(mesh):
    in_specs = (
        P("cfg", "req", None),
        P("cfg", "req", None),
        P("cfg", "req", None),
        P(None, "req"),
        P("req", "cfg"),
        P(),
        P(),
        P(),
        P(),
        P(),
    )
    return jax.shard_map(
        per_device, mesh=mesh, in_specs=in_specs, out_specs=P("req", "cfg"), check_vma=False
    )
```

```python
import functools
import math

import jax
import jax.numpy as jnp
import numpy as np
from jax import lax
from jax.experimental import pallas as pl
from jax.experimental.pallas import tpu as pltpu
from jax.sharding import PartitionSpec as P


HD = 128
ROWS = 512
LATC = 64
TILE = 16
TILES = ROWS // TILE
FAR = 24
REACH = FAR * TILE
SPAN = 2 * ROWS + 128
ACCR = 72
CHUNKS = (56, 60)
ROOM = 28 << 20
masked_score = -1e30
score_scale = math.log2(math.e) / math.sqrt(HD)
rope_theta = 10000.0
MESH = pl.DeviceIdType.MESH
SMEM = pl.BlockSpec(memory_space=pltpu.SMEM)
VMEM = pl.BlockSpec(memory_space=pltpu.VMEM)
ANY = pl.BlockSpec(memory_space=pl.ANY)


def share_static(ta, tb, heads):
    if ta > FAR:
        return 0
    if tb > FAR:
        return heads
    costs = [max(n * ta, (heads - n) * tb) for n in range(heads + 1)]
    return costs.index(min(costs))


def capacity(heads):
    most = 0
    for ta in range(1, TILES + 1):
        for tb in range(1, TILES + 2 - ta):
            n = share_static(ta, tb, heads)
            most = max(most, n * ta, (heads - n) * tb)
    return most


def chunk_tiles(heads):
    cap = capacity(heads)
    if cap >= 150:
        return CHUNKS + (cap - sum(CHUNKS),)
    return (FAR, cap - FAR)


def share(ta, tb, heads):
    best = heads * tb
    chosen = jnp.int32(0)
    for n in range(1, heads + 1):
        cost = jnp.maximum(n * ta, (heads - n) * tb)
        better = cost < best
        best = jnp.where(better, cost, best)
        chosen = jnp.where(better, n, chosen)
    chosen = jnp.where(tb > FAR, heads, chosen)
    return jnp.where(ta > FAR, 0, chosen)


def selector():
    pair_total = HD // 2
    side = HD // 6
    time = pair_total - 2 * side
    axis = np.array([0] * time + [1] * side + [2] * side)
    local = np.array(list(range(time)) + list(range(side)) * 2, np.float32)
    pairs = np.array([time] * time + [side] * (2 * side), np.float32)
    frequency = np.exp(-(local / pairs) * np.float32(math.log(rope_theta))).astype(np.float32)
    table = np.zeros((4, TILE, HD), np.float32)
    for group in range(4):
        for lane in range(HD):
            table[group, axis[lane // 2] * 4 + group, lane] = frequency[lane // 2]
    parts = []
    rest = table
    for _ in range(3):
        part = rest.astype(jnp.bfloat16)
        parts.append(part)
        rest = rest - part.astype(np.float32)
    return np.stack(parts)


def turner():
    table = np.zeros((2 * HD, 2 * HD), np.float32)
    for pair in range(HD):
        table[2 * pair + 1, 2 * pair] = -1.0
        table[2 * pair, 2 * pair + 1] = 1.0
    return table.astype(jnp.bfloat16)


def cdiv(value, unit):
    return (value + unit - 1) // unit


def pack_kernel(heads, chunks, lens_ref, pos_ref, q_ref, k_ref, v_ref, scal_ref, place_ref, *rest):
    count = len(chunks)
    right_refs, left_refs = rest[:count], rest[count : 2 * count]
    rows_in, packed, in_sem, out_sem = rest[2 * count :]
    groups = 4 if heads % 4 == 0 else 1
    width = heads // groups * HD
    loads = []
    for group in range(groups):
        columns = pl.ds(group * width, width)
        for j, source in enumerate((q_ref, k_ref, v_ref)):
            copy = pltpu.make_async_copy(
                source.at[:, :, columns],
                rows_in.at[j, pl.ds(0, TILES), :, columns],
                in_sem.at[group, j],
            )
            copy.start()
            loads.append(copy)
    low = lax.axis_index("req") * ROWS
    high = low + ROWS

    def scan(i, carry):
        end, start_low, end_low, start_high, end_high = carry
        start = end
        end = start + lens_ref[i]
        before_low = start < low
        before_high = start < high
        return (
            end,
            jnp.where(before_low, start, start_low),
            jnp.where(before_low, end, end_low),
            jnp.where(before_high, start, start_high),
            jnp.where(before_high, end, end_high),
        )

    zero = jnp.int32(0)
    _, start_low, end_low, start_high, end_high = lax.fori_loop(
        0, lens_ref.shape[0], scan, (zero, low, low, high, high), unroll=8
    )
    cut_low = end_low > low
    cut_high = end_high > high
    a_low = jnp.where(cut_low, low - start_low, 0)
    b_low = jnp.where(cut_low, end_low - low, 0)
    a_high = jnp.where(cut_high, high - start_high, 0)
    b_high = jnp.where(cut_high, end_high - high, 0)
    n_low = share(cdiv(a_low, TILE), cdiv(b_low, TILE), heads)
    n_high = share(cdiv(a_high, TILE), cdiv(b_high, TILE), heads)
    for i, value in enumerate((a_low, b_low, n_low, a_high, b_high, n_high)):
        scal_ref[i] = value
    scal_ref[6] = zero
    scal_ref[7] = zero

    placed = pos_ref[...].astype(jnp.float32)
    pieces = [placed[a : a + 1, g * HD : (g + 1) * HD] for a in range(3) for g in range(4)]
    pieces.append(jnp.zeros((TILE - 12, HD), jnp.float32))
    place_ref[...] = jnp.concatenate(pieces, axis=0).astype(jnp.bfloat16)

    def pack(direction, first_tile, first_head, tiles, begin, end):
        def one(head, carry):
            columns = pl.ds(pl.multiple_of(head * HD, HD), HD)
            for j in range(3):
                packed[direction, j, pl.ds((head - first_head) * tiles, FAR)] = rows_in[
                    j, pl.ds(first_tile, FAR), :, columns
                ]
            return carry

        lax.fori_loop(begin, end, one, 0)

    ta, tb = cdiv(a_high, TILE), cdiv(b_low, TILE)
    last_right = jnp.where(a_high > 0, n_high, 0)
    first_left = jnp.where(b_low > 0, n_low, heads)
    each = heads // groups
    for group in range(groups):
        for copy in loads[3 * group : 3 * group + 3]:
            copy.wait()
        begin, end = group * each, (group + 1) * each
        pack(0, TILES - ta, 0, ta, begin, jnp.minimum(end, last_right))
        pack(1, 0, n_low, tb, jnp.maximum(begin, first_left), end)
    stores = []
    for direction, targets in enumerate((right_refs, left_refs)):
        begin = 0
        for c, tiles in enumerate(chunks):
            copy = pltpu.make_async_copy(
                packed.at[direction, :, pl.ds(begin, tiles)],
                targets[c].at[:, pl.ds(0, tiles)],
                out_sem.at[direction, c],
            )
            copy.start()
            stores.append(copy)
            begin += tiles
        copy = pltpu.make_async_copy(
            place_ref, targets[0].at[0, chunks[0]], out_sem.at[direction, count]
        )
        copy.start()
        stores.append(copy)
    for copy in stores:
        copy.wait()


def cos_sin(angle):
    turns = jnp.floor(angle * (2.0 / math.pi) + 0.5)
    rest = angle - turns * 1.5703125
    rest = rest - turns * 4.837512969970703125e-4
    rest = rest - turns * 7.54978995489188216e-8
    square = rest * rest
    sine = (-1.9515295891e-4 * square + 8.3321608736e-3) * square - 1.6666654611e-1
    sine = sine * square * rest + rest
    cosine = (2.443315711809948e-5 * square - 1.388731625493765e-3) * square
    cosine = (cosine + 4.166664568298827e-2) * square * square - 0.5 * square + 1.0
    quadrant = turns.astype(jnp.int32)
    odd = (quadrant & 1) == 1
    first, second = jnp.where(odd, sine, cosine), jnp.where(odd, cosine, sine)
    first = jnp.where(((quadrant + 1) & 2) == 2, -first, first)
    return first, jnp.where((quadrant & 2) == 2, -second, second)


def tables(place, select_ref, groups):
    parts = []
    for group in groups:
        angle = None
        for part in range(3):
            term = lax.dot_general(
                place,
                select_ref[part, group],
                (((0,), (0,)), ((), ())),
                preferred_element_type=jnp.float32,
            )
            angle = term if angle is None else angle + term
        parts.append(angle)
    angle = jnp.concatenate(parts, axis=0)
    return cos_sin(angle)


def rotate(q, k, cosine, sine, turn):
    both = jnp.concatenate([q, k], axis=1)
    swapped = jnp.dot(both, turn, preferred_element_type=jnp.float32)
    return (
        q.astype(jnp.float32) * cosine + swapped[:, :HD] * sine,
        k.astype(jnp.float32) * cosine + swapped[:, HD:] * sine,
    )


def attend(q, k, v, bias):
    scores = lax.dot_general(k, q, (((1,), (1,)), ((), ())), preferred_element_type=jnp.float32)
    scores = scores + bias
    top = jnp.max(scores, axis=0, keepdims=True)
    weight = jnp.exp2((scores - top) * score_scale).astype(jnp.bfloat16)
    taller = jnp.concatenate([v.T, jnp.ones((TILE, v.shape[0]), jnp.bfloat16)], axis=0)
    summed = jnp.dot(taller, weight, preferred_element_type=jnp.float32)
    return (summed[:HD] * (1.0 / summed[HD : HD + 1])).astype(jnp.bfloat16)


def add_head(acc_ref, index, lanes, attended, w_block, scale_row):
    weights = (w_block.astype(jnp.float32) * (1.0 + scale_row)).astype(jnp.bfloat16)
    acc_ref[index + (pl.ds(0, LATC), lanes)] += jnp.dot(
        weights, attended, preferred_element_type=jnp.float32
    )
    wide = attended.astype(jnp.float32)
    squared = wide * wide
    total = squared[0:8]
    for part in range(1, HD // 8):
        total = total + squared[part * 8 : part * 8 + 8]
    acc_ref[index + (pl.ds(LATC, 8), lanes)] += total


def local_kernel(
    heads, lens_ref, step_ref, scal_ref, place_ref, select_ref, turn_ref, w_ref, mod_ref,
    q_ref, k_ref, v_ref, turned_ref, acc_ref, steps_ref, shift_ref,
    cos_ref, sin_ref, bias_ref, mine, out_sem,
):
    low = lax.axis_index("req") * ROWS
    lane = lax.broadcasted_iota(jnp.int32, (1, ROWS), 1) + low

    def label(i, carry):
        end, video, step = carry
        end = end + lens_ref[i]
        past = lane >= end
        video = video + past.astype(jnp.int32)
        following = step_ref[jnp.minimum(i + 1, lens_ref.shape[0] - 1)]
        return end, video, jnp.where(past, following, step)

    start = jnp.full((1, ROWS), step_ref[0], jnp.float32)
    _, video, step = lax.fori_loop(
        0, lens_ref.shape[0], label,
        (jnp.int32(0), jnp.zeros((1, ROWS), jnp.int32), start), unroll=8,
    )
    steps_ref[...] = step
    tall = jnp.broadcast_to(video.astype(jnp.float32), (HD, ROWS)).T
    for part in range(ROWS // HD):
        wide = jnp.broadcast_to(
            video[:, part * HD : (part + 1) * HD].astype(jnp.float32), (ROWS, HD)
        )
        bias_ref[:, part * HD : (part + 1) * HD] = jnp.where(tall == wide, 0.0, masked_score)
    cosine, sine = tables(place_ref[...], select_ref, range(4))
    cos_ref[...] = cosine
    sin_ref[...] = sine
    acc_ref[...] = jnp.zeros_like(acc_ref)
    shift = jnp.sum(w_ref[...].astype(jnp.float32) * mod_ref[0:1, :], axis=1, keepdims=True)
    shift_ref[...] = jnp.broadcast_to(shift, (LATC, HD))
    turn = turn_ref[...]
    first = scal_ref[1]
    last = ROWS - scal_ref[3]
    begin = pl.multiple_of(first // HD * HD, HD)
    extent = jnp.where(first < last, cdiv(last, HD) * HD - begin, 0)

    def keep(head, slot):
        return pltpu.make_async_copy(mine.at[slot], turned_ref.at[head], out_sem.at[slot])

    def one(head, carry):
        slot = lax.rem(head, 2)
        columns = pl.ds(pl.multiple_of(head * HD, HD), HD)

        @pl.when(head >= 2)
        def _():
            keep(head, slot).wait()

        q = q_ref[:, columns]
        k = k_ref[:, columns]
        q, k = rotate(q, k, cos_ref[...], sin_ref[...], turn)
        mine[slot, 0] = q.astype(jnp.bfloat16)
        mine[slot, 1] = k.astype(jnp.bfloat16)
        mine[slot, 2] = v_ref[:, columns]
        keep(head, slot).start()
        for width in (128, 256, 384, 512):

            @pl.when(extent == width)
            def _(width=width):
                window = pl.ds(begin, width)
                attended = attend(
                    mine[slot, 0, window], mine[slot, 1, window], mine[slot, 2, window],
                    bias_ref[window, window],
                )
                add_head(acc_ref, (), window, attended, w_ref[:, columns], mod_ref[1:2, columns])

        return carry

    lax.fori_loop(0, heads, one, 0)
    for slot in range(2):
        keep(slot, slot).wait()


def cut_kernel(heads, chunks, c, *refs):
    final = c == len(chunks) - 1
    refs = list(refs)
    scal_ref, select_ref, turn_ref, w_ref, mod_ref, turned_ref = refs[:6]
    del refs[:6]
    here = [i for i in (c - 1, c) if i >= 0]
    sources = [refs[: len(here)], refs[len(here) : 2 * len(here)]]
    del refs[: 2 * len(here)]
    if c == 0:
        acc_ref, table_ref = refs[:2]
        del refs[:2]
    else:
        table_ref, before_ref = refs[:2]
        del refs[:2]
        if final:
            local_ref, own_ref, left_out, right_out = refs[:4]
            del refs[:4]
        else:
            acc_ref = refs.pop(0)
    if final:
        span, recv, bias_ref, loc_sem, recv_sem, acc_ref = refs
    else:
        span, recv, bias_ref, loc_sem, recv_sem = refs
    begins = [sum(chunks[:i]) for i in range(len(chunks) + 1)]
    base = begins[here[0]]
    loads = []
    for side in range(2):
        for i, index in enumerate(here):
            copy = pltpu.make_async_copy(
                sources[side][i].at[:, pl.ds(0, chunks[index])],
                recv.at[side, :, pl.ds(FAR + begins[index] - base, chunks[index])],
                recv_sem.at[side, i],
            )
            copy.start()
            loads.append(copy)
    if c == 0:
        place_copies = []
        for side in range(2):
            copy = pltpu.make_async_copy(
                sources[side][0].at[0, chunks[0]], recv.at[side, 0, 0], recv_sem.at[side, 2]
            )
            copy.start()
            place_copies.append(copy)
    a_low, b_low, n_low = scal_ref[0], scal_ref[1], scal_ref[2]
    a_high, b_high, n_high = scal_ref[3], scal_ref[4], scal_ref[5]
    ta_low, tb_low = cdiv(a_low, TILE), cdiv(b_low, TILE)
    ta_high, tb_high = cdiv(a_high, TILE), cdiv(b_high, TILE)

    def done(limit, tiles, total):
        if limit == 0:
            return jnp.int32(0)
        return jnp.where(tiles > 0, jnp.minimum(total, limit // jnp.maximum(tiles, 1)), 0)

    low_first = done(begins[c], ta_low, n_low)
    low_count = done(begins[c + 1], ta_low, n_low) - low_first
    high_first = done(begins[c], tb_high, heads - n_high)
    high_count = done(begins[c + 1], tb_high, heads - n_high) - high_first
    items = low_count + high_count

    def slot_of(i):
        return jnp.where(i < low_count, low_first + i, high_first + i - low_count)

    def head_of(i):
        return jnp.where(i < low_count, low_first + i, n_high + high_first + i - low_count)

    def fetch(i, buffer):
        rows = pl.ds(pl.multiple_of(jnp.where(i < low_count, ROWS, 0), ROWS), ROWS)
        return pltpu.make_async_copy(
            turned_ref.at[head_of(i)], span.at[buffer, :, rows], loc_sem.at[buffer]
        )

    span[...] = jnp.zeros_like(span)
    shapes = []
    for side, (a, b, ta, tb) in enumerate(
        ((a_low, b_low, ta_low, tb_low), (a_high, b_high, ta_high, tb_high))
    ):
        over = ta + tb > TILES
        skip = jnp.where(over, TILE, 0)
        row = lax.broadcasted_iota(jnp.int32, (ROWS, HD), 0)
        spot = row + skip
        dead = ta * TILE - a
        valid = (spot >= dead) & (spot < ta * TILE + b)
        valid = valid | (over & (row - (ROWS - TILE) >= dead))
        bias_ref[side] = jnp.where(valid, 0.0, masked_score)
        shapes.append((over, ROWS - ta * TILE + skip))
    if c == 0:
        acc_ref[...] = jnp.zeros_like(acc_ref)
        for side, copy in enumerate(place_copies):
            copy.wait()
            groups = range(1, 4) if side == 0 else range(3)
            cosine, sine = tables(recv[side, 0, 0], select_ref, groups)
            table_ref[side, 0] = cosine
            table_ref[side, 1] = sine
    else:
        acc_ref[...] = before_ref[...]

    @pl.when(items > 0)
    def _():
        fetch(jnp.int32(0), 0).start()

    for copy in loads:
        copy.wait()
    turn = turn_ref[...]

    def one(i, carry):
        buffer = lax.rem(i, 2)
        fetch(i, buffer).wait()

        @pl.when(i + 1 < items)
        def _():
            fetch(i + 1, 1 - buffer).start()

        side = (i >= low_count).astype(jnp.int32)
        is_low = side == 0
        slot = slot_of(i)
        head = head_of(i)
        a = jnp.where(is_low, a_low, a_high)
        b = jnp.where(is_low, b_low, b_high)
        ta, tb = cdiv(a, TILE), cdiv(b, TILE)
        offset = jnp.where(is_low, slot * ta + ta, slot * tb + FAR) - base
        first = jnp.where(is_low, REACH - ta * TILE, 0)
        last = jnp.where(is_low, REACH, tb * TILE)
        target = jnp.where(is_low, ROWS - REACH, ROWS)
        for block in range(REACH // HD):
            low, high = block * HD, (block + 1) * HD

            @pl.when((first < high) & (last > low))
            def _(low=low, high=high):
                row = lax.broadcasted_iota(jnp.int32, (HD, HD), 0) + low
                keep = (row >= first) & (row < last)
                tiles = pl.ds(offset + low // TILE, HD // TILE)
                q, k, v = (recv[side, j, tiles].reshape(HD, HD) for j in range(3))
                cosine, sine = table_ref[side, 0, low:high], table_ref[side, 1, low:high]
                q, k = rotate(q, k, cosine, sine, turn)
                rows = pl.ds(pl.multiple_of(target + low, HD), HD)
                for j, x in enumerate((q, k, v.astype(jnp.float32))):
                    span[buffer, j, rows] = jnp.where(keep, x, 0.0).astype(jnp.bfloat16)

        over = ta + tb > TILES

        @pl.when(over)
        def _():
            ahead = pl.ds(pl.multiple_of(ROWS - ta * TILE, TILE), TILE)
            behind = pl.ds(pl.multiple_of(ROWS + (tb - 1) * TILE, TILE), TILE)
            mixed = lax.broadcasted_iota(jnp.int32, (TILE, HD), 0) < b - (tb - 1) * TILE
            for j in range(3):
                merged = jnp.where(
                    mixed, span[buffer, j, behind].astype(jnp.float32), span[buffer, j, ahead].astype(jnp.float32)
                )
                span[buffer, j, behind] = merged.astype(jnp.bfloat16)

        columns = pl.ds(pl.multiple_of(head * HD, HD), HD)
        start = pl.multiple_of(ROWS - ta * TILE + jnp.where(over, TILE, 0), TILE)
        extent = jnp.minimum(ta + tb, TILES) * TILE
        below = 0
        for width in (128, 256, 384, 512):

            @pl.when((extent > below) & (extent <= width))
            def _(width=width):
                rows = pl.ds(start, width)
                bias = jnp.concatenate([bias_ref[side, 0:width]] * (width // HD), axis=1)
                attended = attend(
                    span[buffer, 0, rows], span[buffer, 1, rows], span[buffer, 2, rows], bias
                )
                add_head(
                    acc_ref, (side,), pl.ds(0, width), attended,
                    w_ref[:, columns], mod_ref[1:2, columns],
                )

            below = width
        return carry

    lax.fori_loop(0, items, one, 0)
    if final:
        halves = []
        lane = lax.broadcasted_iota(jnp.int32, (ACCR, 2 * ROWS), 1)
        for side, (over, start) in enumerate(shapes):
            placed = jnp.concatenate([acc_ref[side], jnp.zeros((ACCR, ROWS), jnp.float32)], axis=1)
            placed = pltpu.roll(placed, start, 1)
            swapped = jnp.concatenate([placed[:, ROWS:], placed[:, :ROWS]], axis=1)
            extra = over & (lane < start)
            placed = jnp.where(extra, swapped, placed)
            halves.append((placed[:, :ROWS], placed[:, ROWS:]))
        lane = lax.broadcasted_iota(jnp.int32, (ACCR, ROWS), 1)
        own = jnp.where(lane < b_low, halves[0][1], 0.0)
        own = own + jnp.where(lane >= ROWS - a_high, halves[1][0], 0.0)
        own_ref[...] = own + jnp.where((lane >= b_low) & (lane < ROWS - a_high), local_ref[...], 0.0)
        back = jnp.where(lane >= ROWS - a_low, halves[0][0], 0.0)
        left_out[...] = back[:, ROWS - REACH :]
        back = jnp.where(lane < b_high, halves[1][1], 0.0)
        right_out[...] = back[:, :REACH]


def finish_kernel(
    features, ring, own_ref, left_ref, right_ref, shift_ref, guide_ref, out_ref,
    from_left, from_right, velocity, other, send_sem, recv_sem,
):
    me = lax.axis_index("req")
    parity = lax.axis_index("cfg")
    left, right = lax.rem(me + ring - 1, ring), lax.rem(me + 1, ring)
    partner = {"cfg": 1 - parity}
    barrier = pltpu.get_barrier_semaphore()
    for target in ({"req": left}, {"req": right}, partner):
        pl.semaphore_signal(barrier, inc=1, device_id=target, device_id_type=MESH)
    pl.semaphore_wait(barrier, 3)
    to_left = pltpu.make_async_remote_copy(
        left_ref, from_right, send_sem.at[0], recv_sem.at[0],
        device_id={"req": left}, device_id_type=MESH,
    )
    to_left.start()
    to_right = pltpu.make_async_remote_copy(
        right_ref, from_left, send_sem.at[1], recv_sem.at[1],
        device_id={"req": right}, device_id_type=MESH,
    )
    to_right.start()
    to_left.wait()
    to_right.wait()
    none = jnp.zeros((ACCR, ROWS - REACH), jnp.float32)
    total = own_ref[...]
    total = total + jnp.concatenate([none, from_right[...]], axis=1)
    total = total + jnp.concatenate([from_left[...], none], axis=1)
    square = jnp.sum(total[LATC:], axis=0, keepdims=True)
    inverse = lax.rsqrt(square * (1.0 / features) + 1e-06)
    velocity[...] = total[:LATC] * inverse + shift_ref[:, 0:1]
    half = LATC // 2
    give = pltpu.make_async_remote_copy(
        velocity.at[pl.ds(pl.multiple_of((1 - parity) * half, half), half)],
        other, send_sem.at[2], recv_sem.at[2], device_id=partner, device_id_type=MESH,
    )
    give.start()
    kept = velocity[pl.ds(pl.multiple_of(parity * half, half), half)]
    give.wait()
    theirs = other[...]
    conditional = jnp.where(parity == 0, kept, theirs)
    unconditional = jnp.where(parity == 0, theirs, kept)
    out_ref[...] = unconditional + guide_ref[0] * (conditional - unconditional)


def moved(value, step, ring):
    return lax.ppermute(value, "req", [(i, (i + step) % ring) for i in range(ring)])


def per_device(
    query_rows, key_rows, value_rows, positions, latents, w_head, modulation, guide_scale,
    step_sizes, lengths,
):
    features = query_rows.shape[2]
    heads = features // HD
    ring = lax.axis_size("req")
    chunks = chunk_tiles(heads)
    count = len(chunks)
    bf16, f32 = jnp.bfloat16, jnp.float32
    sized = jax.ShapeDtypeStruct
    q, k, v = query_rows[0], key_rows[0], value_rows[0]

    def tiled(x):
        return x.reshape(TILES, TILE, features)

    shapes = [sized((3, t + (i == 0), TILE, HD), bf16) for i, t in enumerate(chunks)]
    packed_tiles = sum(chunks) + FAR
    outs = pl.pallas_call(
        functools.partial(pack_kernel, heads, chunks),
        out_shape=[sized((8,), jnp.int32), sized((TILE, HD), bf16)] + shapes + shapes,
        in_specs=[SMEM, VMEM, ANY, ANY, ANY],
        out_specs=[SMEM, VMEM] + [ANY] * (2 * count),
        scratch_shapes=[
            pltpu.VMEM((3, TILES + FAR, TILE, features), bf16),
            pltpu.VMEM((2, 3, packed_tiles, TILE, HD), bf16),
            pltpu.SemaphoreType.DMA((4, 3)),
            pltpu.SemaphoreType.DMA((2, count + 1)),
        ],
        name="pack",
    )(lengths, positions, tiled(q), tiled(k), tiled(v))
    scal, place = outs[:2]
    to_right, to_left = outs[2 : 2 + count], outs[2 + count :]
    from_left = []
    from_right = []
    for c in range(count):
        from_left.append(moved(to_right[c], 1, ring))
        from_right.append(moved(to_left[c], -1, ring))

    select = jnp.asarray(selector())
    turn = jnp.asarray(turner())
    w_turned = w_head.T
    pair_ops = ROWS * ROWS * HD * 4
    turned, local_acc, steps, shift = pl.pallas_call(
        functools.partial(local_kernel, heads),
        out_shape=[
            sized((heads, 3, ROWS, HD), bf16),
            sized((ACCR, ROWS), f32),
            sized((1, ROWS), f32),
            sized((LATC, HD), f32),
        ],
        in_specs=[SMEM, SMEM, SMEM] + [VMEM] * 8,
        out_specs=[ANY, VMEM, VMEM, VMEM],
        scratch_shapes=[
            pltpu.VMEM((ROWS, HD), f32),
            pltpu.VMEM((ROWS, HD), f32),
            pltpu.VMEM((ROWS, ROWS), f32),
            pltpu.VMEM((2, 3, ROWS, HD), bf16),
            pltpu.SemaphoreType.DMA((2,)),
        ],
        cost_estimate=pl.CostEstimate(
            flops=heads * pair_ops, bytes_accessed=6 * ROWS * features * 2, transcendentals=0
        ),
        compiler_params=pltpu.CompilerParams(vmem_limit_bytes=ROOM),
        name="local",
    )(
        lengths, step_sizes, scal, place, select, turn, w_turned, modulation,
        q, k, v,
    )

    acc = table = None
    for c in range(count):
        final = c == count - 1
        here = [i for i in (c - 1, c) if i >= 0]
        operands = [scal, select, turn, w_turned, modulation, turned]
        specs = [SMEM, VMEM, VMEM, VMEM, VMEM, ANY]
        operands += [from_left[i] for i in here] + [from_right[i] for i in here]
        specs += [ANY] * (2 * len(here))
        if c > 0:
            operands += [table, acc]
            specs += [VMEM, VMEM]
        acc_shape = sized((2, ACCR, ROWS), f32)
        if final:
            operands.append(local_acc)
            specs.append(VMEM)
            out_shape = [
                sized((ACCR, ROWS), f32),
                sized((ACCR, REACH), f32),
                sized((ACCR, REACH), f32),
            ]
        elif c == 0:
            out_shape = [acc_shape, sized((2, 2, REACH, HD), f32)]
        else:
            out_shape = [acc_shape]
        scratch = [
            pltpu.VMEM((2, 3, SPAN, HD), bf16),
            pltpu.VMEM((2, 3, 2 * FAR + sum(chunks[i] for i in here), TILE, HD), bf16),
            pltpu.VMEM((2, ROWS, HD), f32),
            pltpu.SemaphoreType.DMA((2,)),
            pltpu.SemaphoreType.DMA((2, 3)),
        ]
        if final:
            scratch.append(pltpu.VMEM((2, ACCR, ROWS), f32))
        results = pl.pallas_call(
            functools.partial(cut_kernel, heads, chunks, c),
            out_shape=out_shape,
            in_specs=specs,
            out_specs=[VMEM] * len(out_shape),
            scratch_shapes=scratch,
            cost_estimate=pl.CostEstimate(
                flops=heads * pair_ops // count, bytes_accessed=4 << 20, transcendentals=0
            ),
            compiler_params=pltpu.CompilerParams(vmem_limit_bytes=ROOM),
        )(*operands)
        if final:
            own, back_left, back_right = results
        elif c == 0:
            acc, table = results
        else:
            (acc,) = results

    guided = pl.pallas_call(
        functools.partial(finish_kernel, features, ring),
        out_shape=sized((LATC // 2, ROWS), f32),
        in_specs=[VMEM, VMEM, VMEM, VMEM, SMEM],
        out_specs=VMEM,
        scratch_shapes=[
            pltpu.VMEM((ACCR, REACH), f32),
            pltpu.VMEM((ACCR, REACH), f32),
            pltpu.VMEM((LATC, ROWS), f32),
            pltpu.VMEM((LATC // 2, ROWS), f32),
            pltpu.SemaphoreType.DMA((3,)),
            pltpu.SemaphoreType.DMA((3,)),
        ],
        compiler_params=pltpu.CompilerParams(collective_id=0, has_side_effects=True),
        name="finish",
    )(own, back_left, back_right, shift, guide_scale)
    return (latents.T + steps * guided).T


def solution(mesh):
    in_specs = (
        P("cfg", "req", None),
        P("cfg", "req", None),
        P("cfg", "req", None),
        P(None, "req"),
        P("req", "cfg"),
        P(),
        P(),
        P(),
        P(),
        P(),
    )
    return jax.shard_map(
        per_device, mesh=mesh, in_specs=in_specs, out_specs=P("req", "cfg"), check_vma=False
    )
```

```python
import functools
import math

import jax
import jax.numpy as jnp
import numpy as np
from jax import lax
from jax.experimental import pallas as pl
from jax.experimental.pallas import tpu as pltpu
from jax.sharding import PartitionSpec as P


HD = 128
ROWS = 512
LATC = 64
TILE = 16
TILES = ROWS // TILE
FAR = 24
REACH = FAR * TILE
SPAN = 2 * ROWS + 128
ACCR = 72
CHUNKS = (80,)
ROOM = 28 << 20
masked_score = -1e30
score_scale = math.log2(math.e) / math.sqrt(HD)
rope_theta = 10000.0
MESH = pl.DeviceIdType.MESH
SMEM = pl.BlockSpec(memory_space=pltpu.SMEM)
VMEM = pl.BlockSpec(memory_space=pltpu.VMEM)
ANY = pl.BlockSpec(memory_space=pl.ANY)


def share_static(ta, tb, heads):
    if ta > FAR:
        return 0
    if tb > FAR:
        return heads
    costs = [max(n * ta, (heads - n) * tb) for n in range(heads + 1)]
    return costs.index(min(costs))


def capacity(heads):
    most = 0
    for ta in range(1, TILES + 1):
        for tb in range(1, TILES + 2 - ta):
            n = share_static(ta, tb, heads)
            most = max(most, n * ta, (heads - n) * tb)
    return most


def chunk_tiles(heads):
    cap = capacity(heads)
    if cap >= 150:
        return CHUNKS + (cap - sum(CHUNKS),)
    return (FAR, cap - FAR)


def share(ta, tb, heads):
    best = heads * tb
    chosen = jnp.int32(0)
    for n in range(1, heads + 1):
        cost = jnp.maximum(n * ta, (heads - n) * tb)
        better = cost < best
        best = jnp.where(better, cost, best)
        chosen = jnp.where(better, n, chosen)
    chosen = jnp.where(tb > FAR, heads, chosen)
    return jnp.where(ta > FAR, 0, chosen)


def selector():
    pair_total = HD // 2
    side = HD // 6
    time = pair_total - 2 * side
    axis = np.array([0] * time + [1] * side + [2] * side)
    local = np.array(list(range(time)) + list(range(side)) * 2, np.float32)
    pairs = np.array([time] * time + [side] * (2 * side), np.float32)
    frequency = np.exp(-(local / pairs) * np.float32(math.log(rope_theta))).astype(np.float32)
    table = np.zeros((4, TILE, HD), np.float32)
    for group in range(4):
        for lane in range(HD):
            table[group, axis[lane // 2] * 4 + group, lane] = frequency[lane // 2]
    parts = []
    rest = table
    for _ in range(3):
        part = rest.astype(jnp.bfloat16)
        parts.append(part)
        rest = rest - part.astype(np.float32)
    return np.stack(parts)


def turner():
    table = np.zeros((2 * HD, 2 * HD), np.float32)
    for pair in range(HD):
        table[2 * pair + 1, 2 * pair] = -1.0
        table[2 * pair, 2 * pair + 1] = 1.0
    return table.astype(jnp.bfloat16)


def cdiv(value, unit):
    return (value + unit - 1) // unit


def pack_kernel(heads, chunks, lens_ref, pos_ref, q_ref, k_ref, v_ref, scal_ref, place_ref, *rest):
    count = len(chunks)
    right_refs, left_refs = rest[:count], rest[count : 2 * count]
    rows_in, packed, in_sem, out_sem = rest[2 * count :]
    groups = 4 if heads % 4 == 0 else 1
    width = heads // groups * HD
    loads = []
    for group in range(groups):
        columns = pl.ds(group * width, width)
        for j, source in enumerate((q_ref, k_ref, v_ref)):
            copy = pltpu.make_async_copy(
                source.at[:, :, columns],
                rows_in.at[j, pl.ds(0, TILES), :, columns],
                in_sem.at[group, j],
            )
            copy.start()
            loads.append(copy)
    low = lax.axis_index("req") * ROWS
    high = low + ROWS

    def scan(i, carry):
        end, start_low, end_low, start_high, end_high = carry
        start = end
        end = start + lens_ref[i]
        before_low = start < low
        before_high = start < high
        return (
            end,
            jnp.where(before_low, start, start_low),
            jnp.where(before_low, end, end_low),
            jnp.where(before_high, start, start_high),
            jnp.where(before_high, end, end_high),
        )

    zero = jnp.int32(0)
    _, start_low, end_low, start_high, end_high = lax.fori_loop(
        0, lens_ref.shape[0], scan, (zero, low, low, high, high), unroll=8
    )
    cut_low = end_low > low
    cut_high = end_high > high
    a_low = jnp.where(cut_low, low - start_low, 0)
    b_low = jnp.where(cut_low, end_low - low, 0)
    a_high = jnp.where(cut_high, high - start_high, 0)
    b_high = jnp.where(cut_high, end_high - high, 0)
    n_low = share(cdiv(a_low, TILE), cdiv(b_low, TILE), heads)
    n_high = share(cdiv(a_high, TILE), cdiv(b_high, TILE), heads)
    for i, value in enumerate((a_low, b_low, n_low, a_high, b_high, n_high)):
        scal_ref[i] = value
    scal_ref[6] = zero
    scal_ref[7] = zero

    placed = pos_ref[...].astype(jnp.float32)
    pieces = [placed[a : a + 1, g * HD : (g + 1) * HD] for a in range(3) for g in range(4)]
    pieces.append(jnp.zeros((TILE - 12, HD), jnp.float32))
    place_ref[...] = jnp.concatenate(pieces, axis=0).astype(jnp.bfloat16)

    def pack(direction, first_tile, first_head, tiles, begin, end):
        def one(head, carry):
            columns = pl.ds(pl.multiple_of(head * HD, HD), HD)
            for j in range(3):
                packed[direction, j, pl.ds((head - first_head) * tiles, FAR)] = rows_in[
                    j, pl.ds(first_tile, FAR), :, columns
                ]
            return carry

        lax.fori_loop(begin, end, one, 0)

    ta, tb = cdiv(a_high, TILE), cdiv(b_low, TILE)
    last_right = jnp.where(a_high > 0, n_high, 0)
    first_left = jnp.where(b_low > 0, n_low, heads)
    each = heads // groups
    for group in range(groups):
        for copy in loads[3 * group : 3 * group + 3]:
            copy.wait()
        begin, end = group * each, (group + 1) * each
        pack(0, TILES - ta, 0, ta, begin, jnp.minimum(end, last_right))
        pack(1, 0, n_low, tb, jnp.maximum(begin, first_left), end)
    stores = []
    for direction, targets in enumerate((right_refs, left_refs)):
        begin = 0
        for c, tiles in enumerate(chunks):
            copy = pltpu.make_async_copy(
                packed.at[direction, :, pl.ds(begin, tiles)],
                targets[c].at[:, pl.ds(0, tiles)],
                out_sem.at[direction, c],
            )
            copy.start()
            stores.append(copy)
            begin += tiles
        copy = pltpu.make_async_copy(
            place_ref, targets[0].at[0, chunks[0]], out_sem.at[direction, count]
        )
        copy.start()
        stores.append(copy)
    for copy in stores:
        copy.wait()


def cos_sin(angle):
    turns = jnp.floor(angle * (2.0 / math.pi) + 0.5)
    rest = angle - turns * 1.5703125
    rest = rest - turns * 4.837512969970703125e-4
    rest = rest - turns * 7.54978995489188216e-8
    square = rest * rest
    sine = (-1.9515295891e-4 * square + 8.3321608736e-3) * square - 1.6666654611e-1
    sine = sine * square * rest + rest
    cosine = (2.443315711809948e-5 * square - 1.388731625493765e-3) * square
    cosine = (cosine + 4.166664568298827e-2) * square * square - 0.5 * square + 1.0
    quadrant = turns.astype(jnp.int32)
    odd = (quadrant & 1) == 1
    first, second = jnp.where(odd, sine, cosine), jnp.where(odd, cosine, sine)
    first = jnp.where(((quadrant + 1) & 2) == 2, -first, first)
    return first, jnp.where((quadrant & 2) == 2, -second, second)


def tables(place, select_ref, groups):
    parts = []
    for group in groups:
        angle = None
        for part in range(3):
            term = lax.dot_general(
                place,
                select_ref[part, group],
                (((0,), (0,)), ((), ())),
                preferred_element_type=jnp.float32,
            )
            angle = term if angle is None else angle + term
        parts.append(angle)
    angle = jnp.concatenate(parts, axis=0)
    return cos_sin(angle)


def rotate(q, k, cosine, sine, turn):
    both = jnp.concatenate([q, k], axis=1)
    swapped = jnp.dot(both, turn, preferred_element_type=jnp.float32)
    return (
        q.astype(jnp.float32) * cosine + swapped[:, :HD] * sine,
        k.astype(jnp.float32) * cosine + swapped[:, HD:] * sine,
    )


def attend(q, k, v, bias):
    scores = lax.dot_general(k, q, (((1,), (1,)), ((), ())), preferred_element_type=jnp.float32)
    scores = scores + bias
    top = jnp.max(scores, axis=0, keepdims=True)
    weight = jnp.exp2((scores - top) * score_scale).astype(jnp.bfloat16)
    taller = jnp.concatenate([v.T, jnp.ones((TILE, v.shape[0]), jnp.bfloat16)], axis=0)
    summed = jnp.dot(taller, weight, preferred_element_type=jnp.float32)
    return (summed[:HD] * (1.0 / summed[HD : HD + 1])).astype(jnp.bfloat16)


def add_head(acc_ref, index, lanes, attended, w_block, scale_row):
    weights = (w_block.astype(jnp.float32) * (1.0 + scale_row)).astype(jnp.bfloat16)
    acc_ref[index + (pl.ds(0, LATC), lanes)] += jnp.dot(
        weights, attended, preferred_element_type=jnp.float32
    )
    wide = attended.astype(jnp.float32)
    squared = wide * wide
    total = squared[0:8]
    for part in range(1, HD // 8):
        total = total + squared[part * 8 : part * 8 + 8]
    acc_ref[index + (pl.ds(LATC, 8), lanes)] += total


def local_kernel(
    heads, lens_ref, step_ref, scal_ref, place_ref, select_ref, turn_ref, w_ref, mod_ref,
    q_ref, k_ref, v_ref, turned_ref, acc_ref, steps_ref, shift_ref,
    cos_ref, sin_ref, bias_ref, mine, out_sem,
):
    low = lax.axis_index("req") * ROWS
    lane = lax.broadcasted_iota(jnp.int32, (1, ROWS), 1) + low

    def label(i, carry):
        end, video, step = carry
        end = end + lens_ref[i]
        past = lane >= end
        video = video + past.astype(jnp.int32)
        following = step_ref[jnp.minimum(i + 1, lens_ref.shape[0] - 1)]
        return end, video, jnp.where(past, following, step)

    start = jnp.full((1, ROWS), step_ref[0], jnp.float32)
    _, video, step = lax.fori_loop(
        0, lens_ref.shape[0], label,
        (jnp.int32(0), jnp.zeros((1, ROWS), jnp.int32), start), unroll=8,
    )
    steps_ref[...] = step
    tall = jnp.broadcast_to(video.astype(jnp.float32), (HD, ROWS)).T
    for part in range(ROWS // HD):
        wide = jnp.broadcast_to(
            video[:, part * HD : (part + 1) * HD].astype(jnp.float32), (ROWS, HD)
        )
        bias_ref[:, part * HD : (part + 1) * HD] = jnp.where(tall == wide, 0.0, masked_score)
    cosine, sine = tables(place_ref[...], select_ref, range(4))
    cos_ref[...] = cosine
    sin_ref[...] = sine
    acc_ref[...] = jnp.zeros_like(acc_ref)
    shift = jnp.sum(w_ref[...].astype(jnp.float32) * mod_ref[0:1, :], axis=1, keepdims=True)
    shift_ref[...] = jnp.broadcast_to(shift, (LATC, HD))
    turn = turn_ref[...]
    first = scal_ref[1]
    last = ROWS - scal_ref[3]
    begin = pl.multiple_of(first // HD * HD, HD)
    extent = jnp.where(first < last, cdiv(last, HD) * HD - begin, 0)

    def keep(head, slot):
        return pltpu.make_async_copy(mine.at[slot], turned_ref.at[head], out_sem.at[slot])

    def one(head, carry):
        slot = lax.rem(head, 2)
        columns = pl.ds(pl.multiple_of(head * HD, HD), HD)

        @pl.when(head >= 2)
        def _():
            keep(head, slot).wait()

        q = q_ref[:, columns]
        k = k_ref[:, columns]
        q, k = rotate(q, k, cos_ref[...], sin_ref[...], turn)
        mine[slot, 0] = q.astype(jnp.bfloat16)
        mine[slot, 1] = k.astype(jnp.bfloat16)
        mine[slot, 2] = v_ref[:, columns]
        keep(head, slot).start()
        for width in (128, 256, 384, 512):

            @pl.when(extent == width)
            def _(width=width):
                window = pl.ds(begin, width)
                attended = attend(
                    mine[slot, 0, window], mine[slot, 1, window], mine[slot, 2, window],
                    bias_ref[window, window],
                )
                add_head(acc_ref, (), window, attended, w_ref[:, columns], mod_ref[1:2, columns])

        return carry

    lax.fori_loop(0, heads, one, 0)
    for slot in range(2):
        keep(slot, slot).wait()


def cut_kernel(heads, chunks, c, *refs):
    final = c == len(chunks) - 1
    refs = list(refs)
    scal_ref, select_ref, turn_ref, w_ref, mod_ref, turned_ref = refs[:6]
    del refs[:6]
    here = [i for i in (c - 1, c) if i >= 0]
    sources = [refs[: len(here)], refs[len(here) : 2 * len(here)]]
    del refs[: 2 * len(here)]
    if c == 0:
        acc_ref, table_ref = refs[:2]
        del refs[:2]
    else:
        table_ref, before_ref = refs[:2]
        del refs[:2]
        if final:
            local_ref, own_ref, left_out, right_out = refs[:4]
            del refs[:4]
        else:
            acc_ref = refs.pop(0)
    if final:
        span, recv, bias_ref, loc_sem, recv_sem, acc_ref = refs
    else:
        span, recv, bias_ref, loc_sem, recv_sem = refs
    begins = [sum(chunks[:i]) for i in range(len(chunks) + 1)]
    base = begins[here[0]]
    loads = []
    for side in range(2):
        for i, index in enumerate(here):
            copy = pltpu.make_async_copy(
                sources[side][i].at[:, pl.ds(0, chunks[index])],
                recv.at[side, :, pl.ds(FAR + begins[index] - base, chunks[index])],
                recv_sem.at[side, i],
            )
            copy.start()
            loads.append(copy)
    if c == 0:
        place_copies = []
        for side in range(2):
            copy = pltpu.make_async_copy(
                sources[side][0].at[0, chunks[0]], recv.at[side, 0, 0], recv_sem.at[side, 2]
            )
            copy.start()
            place_copies.append(copy)
    a_low, b_low, n_low = scal_ref[0], scal_ref[1], scal_ref[2]
    a_high, b_high, n_high = scal_ref[3], scal_ref[4], scal_ref[5]
    ta_low, tb_low = cdiv(a_low, TILE), cdiv(b_low, TILE)
    ta_high, tb_high = cdiv(a_high, TILE), cdiv(b_high, TILE)

    def done(limit, tiles, total):
        if limit == 0:
            return jnp.int32(0)
        return jnp.where(tiles > 0, jnp.minimum(total, limit // jnp.maximum(tiles, 1)), 0)

    low_first = done(begins[c], ta_low, n_low)
    low_count = done(begins[c + 1], ta_low, n_low) - low_first
    high_first = done(begins[c], tb_high, heads - n_high)
    high_count = done(begins[c + 1], tb_high, heads - n_high) - high_first
    items = low_count + high_count

    def slot_of(i):
        return jnp.where(i < low_count, low_first + i, high_first + i - low_count)

    def head_of(i):
        return jnp.where(i < low_count, low_first + i, n_high + high_first + i - low_count)

    def fetch(i, buffer):
        rows = pl.ds(pl.multiple_of(jnp.where(i < low_count, ROWS, 0), ROWS), ROWS)
        return pltpu.make_async_copy(
            turned_ref.at[head_of(i)], span.at[buffer, :, rows], loc_sem.at[buffer]
        )

    span[...] = jnp.zeros_like(span)
    shapes = []
    for side, (a, b, ta, tb) in enumerate(
        ((a_low, b_low, ta_low, tb_low), (a_high, b_high, ta_high, tb_high))
    ):
        over = ta + tb > TILES
        skip = jnp.where(over, TILE, 0)
        row = lax.broadcasted_iota(jnp.int32, (ROWS, HD), 0)
        spot = row + skip
        dead = ta * TILE - a
        valid = (spot >= dead) & (spot < ta * TILE + b)
        valid = valid | (over & (row - (ROWS - TILE) >= dead))
        bias_ref[side] = jnp.where(valid, 0.0, masked_score)
        shapes.append((over, ROWS - ta * TILE + skip))
    if c == 0:
        acc_ref[...] = jnp.zeros_like(acc_ref)
        for side, copy in enumerate(place_copies):
            copy.wait()
            groups = range(1, 4) if side == 0 else range(3)
            cosine, sine = tables(recv[side, 0, 0], select_ref, groups)
            table_ref[side, 0] = cosine
            table_ref[side, 1] = sine
    else:
        acc_ref[...] = before_ref[...]

    @pl.when(items > 0)
    def _():
        fetch(jnp.int32(0), 0).start()

    for copy in loads:
        copy.wait()
    turn = turn_ref[...]

    def one(i, carry):
        buffer = lax.rem(i, 2)
        fetch(i, buffer).wait()

        @pl.when(i + 1 < items)
        def _():
            fetch(i + 1, 1 - buffer).start()

        side = (i >= low_count).astype(jnp.int32)
        is_low = side == 0
        slot = slot_of(i)
        head = head_of(i)
        a = jnp.where(is_low, a_low, a_high)
        b = jnp.where(is_low, b_low, b_high)
        ta, tb = cdiv(a, TILE), cdiv(b, TILE)
        offset = jnp.where(is_low, slot * ta + ta, slot * tb + FAR) - base
        first = jnp.where(is_low, REACH - ta * TILE, 0)
        last = jnp.where(is_low, REACH, tb * TILE)
        target = jnp.where(is_low, ROWS - REACH, ROWS)
        for block in range(REACH // HD):
            low, high = block * HD, (block + 1) * HD

            @pl.when((first < high) & (last > low))
            def _(low=low, high=high):
                row = lax.broadcasted_iota(jnp.int32, (HD, HD), 0) + low
                keep = (row >= first) & (row < last)
                tiles = pl.ds(offset + low // TILE, HD // TILE)
                q, k, v = (recv[side, j, tiles].reshape(HD, HD) for j in range(3))
                cosine, sine = table_ref[side, 0, low:high], table_ref[side, 1, low:high]
                q, k = rotate(q, k, cosine, sine, turn)
                rows = pl.ds(pl.multiple_of(target + low, HD), HD)
                for j, x in enumerate((q, k, v.astype(jnp.float32))):
                    span[buffer, j, rows] = jnp.where(keep, x, 0.0).astype(jnp.bfloat16)

        over = ta + tb > TILES

        @pl.when(over)
        def _():
            ahead = pl.ds(pl.multiple_of(ROWS - ta * TILE, TILE), TILE)
            behind = pl.ds(pl.multiple_of(ROWS + (tb - 1) * TILE, TILE), TILE)
            mixed = lax.broadcasted_iota(jnp.int32, (TILE, HD), 0) < b - (tb - 1) * TILE
            for j in range(3):
                merged = jnp.where(
                    mixed, span[buffer, j, behind].astype(jnp.float32), span[buffer, j, ahead].astype(jnp.float32)
                )
                span[buffer, j, behind] = merged.astype(jnp.bfloat16)

        columns = pl.ds(pl.multiple_of(head * HD, HD), HD)
        start = pl.multiple_of(ROWS - ta * TILE + jnp.where(over, TILE, 0), TILE)
        extent = jnp.minimum(ta + tb, TILES) * TILE
        below = 0
        for width in (128, 256, 384, 512):

            @pl.when((extent > below) & (extent <= width))
            def _(width=width):
                rows = pl.ds(start, width)
                bias = jnp.concatenate([bias_ref[side, 0:width]] * (width // HD), axis=1)
                attended = attend(
                    span[buffer, 0, rows], span[buffer, 1, rows], span[buffer, 2, rows], bias
                )
                add_head(
                    acc_ref, (side,), pl.ds(0, width), attended,
                    w_ref[:, columns], mod_ref[1:2, columns],
                )

            below = width
        return carry

    lax.fori_loop(0, items, one, 0)
    if final:
        halves = []
        lane = lax.broadcasted_iota(jnp.int32, (ACCR, 2 * ROWS), 1)
        for side, (over, start) in enumerate(shapes):
            placed = jnp.concatenate([acc_ref[side], jnp.zeros((ACCR, ROWS), jnp.float32)], axis=1)
            placed = pltpu.roll(placed, start, 1)
            swapped = jnp.concatenate([placed[:, ROWS:], placed[:, :ROWS]], axis=1)
            extra = over & (lane < start)
            placed = jnp.where(extra, swapped, placed)
            halves.append((placed[:, :ROWS], placed[:, ROWS:]))
        lane = lax.broadcasted_iota(jnp.int32, (ACCR, ROWS), 1)
        own = jnp.where(lane < b_low, halves[0][1], 0.0)
        own = own + jnp.where(lane >= ROWS - a_high, halves[1][0], 0.0)
        own_ref[...] = own + jnp.where((lane >= b_low) & (lane < ROWS - a_high), local_ref[...], 0.0)
        back = jnp.where(lane >= ROWS - a_low, halves[0][0], 0.0)
        left_out[...] = back[:, ROWS - REACH :]
        back = jnp.where(lane < b_high, halves[1][1], 0.0)
        right_out[...] = back[:, :REACH]


def finish_kernel(
    features, ring, own_ref, left_ref, right_ref, shift_ref, guide_ref, out_ref,
    from_left, from_right, velocity, other, send_sem, recv_sem,
):
    me = lax.axis_index("req")
    parity = lax.axis_index("cfg")
    left, right = lax.rem(me + ring - 1, ring), lax.rem(me + 1, ring)
    partner = {"cfg": 1 - parity}
    barrier = pltpu.get_barrier_semaphore()
    for target in ({"req": left}, {"req": right}, partner):
        pl.semaphore_signal(barrier, inc=1, device_id=target, device_id_type=MESH)
    pl.semaphore_wait(barrier, 3)
    to_left = pltpu.make_async_remote_copy(
        left_ref, from_right, send_sem.at[0], recv_sem.at[0],
        device_id={"req": left}, device_id_type=MESH,
    )
    to_left.start()
    to_right = pltpu.make_async_remote_copy(
        right_ref, from_left, send_sem.at[1], recv_sem.at[1],
        device_id={"req": right}, device_id_type=MESH,
    )
    to_right.start()
    to_left.wait()
    to_right.wait()
    none = jnp.zeros((ACCR, ROWS - REACH), jnp.float32)
    total = own_ref[...]
    total = total + jnp.concatenate([none, from_right[...]], axis=1)
    total = total + jnp.concatenate([from_left[...], none], axis=1)
    square = jnp.sum(total[LATC:], axis=0, keepdims=True)
    inverse = lax.rsqrt(square * (1.0 / features) + 1e-06)
    velocity[...] = total[:LATC] * inverse + shift_ref[:, 0:1]
    half = LATC // 2
    give = pltpu.make_async_remote_copy(
        velocity.at[pl.ds(pl.multiple_of((1 - parity) * half, half), half)],
        other, send_sem.at[2], recv_sem.at[2], device_id=partner, device_id_type=MESH,
    )
    give.start()
    kept = velocity[pl.ds(pl.multiple_of(parity * half, half), half)]
    give.wait()
    theirs = other[...]
    conditional = jnp.where(parity == 0, kept, theirs)
    unconditional = jnp.where(parity == 0, theirs, kept)
    out_ref[...] = unconditional + guide_ref[0] * (conditional - unconditional)


def moved(value, step, ring):
    return lax.ppermute(value, "req", [(i, (i + step) % ring) for i in range(ring)])


def per_device(
    query_rows, key_rows, value_rows, positions, latents, w_head, modulation, guide_scale,
    step_sizes, lengths,
):
    features = query_rows.shape[2]
    heads = features // HD
    ring = lax.axis_size("req")
    chunks = chunk_tiles(heads)
    count = len(chunks)
    bf16, f32 = jnp.bfloat16, jnp.float32
    sized = jax.ShapeDtypeStruct
    q, k, v = query_rows[0], key_rows[0], value_rows[0]

    def tiled(x):
        return x.reshape(TILES, TILE, features)

    shapes = [sized((3, t + (i == 0), TILE, HD), bf16) for i, t in enumerate(chunks)]
    packed_tiles = sum(chunks) + FAR
    outs = pl.pallas_call(
        functools.partial(pack_kernel, heads, chunks),
        out_shape=[sized((8,), jnp.int32), sized((TILE, HD), bf16)] + shapes + shapes,
        in_specs=[SMEM, VMEM, ANY, ANY, ANY],
        out_specs=[SMEM, VMEM] + [ANY] * (2 * count),
        scratch_shapes=[
            pltpu.VMEM((3, TILES + FAR, TILE, features), bf16),
            pltpu.VMEM((2, 3, packed_tiles, TILE, HD), bf16),
            pltpu.SemaphoreType.DMA((4, 3)),
            pltpu.SemaphoreType.DMA((2, count + 1)),
        ],
        compiler_params=pltpu.CompilerParams(vmem_limit_bytes=56 << 20),
        name="pack",
    )(lengths, positions, tiled(q), tiled(k), tiled(v))
    scal, place = outs[:2]
    to_right, to_left = outs[2 : 2 + count], outs[2 + count :]
    from_left = []
    from_right = []
    for c in range(count):
        from_left.append(moved(to_right[c], 1, ring))
        from_right.append(moved(to_left[c], -1, ring))

    select = jnp.asarray(selector())
    turn = jnp.asarray(turner())
    w_turned = w_head.T
    pair_ops = ROWS * ROWS * HD * 4
    turned, local_acc, steps, shift = pl.pallas_call(
        functools.partial(local_kernel, heads),
        out_shape=[
            sized((heads, 3, ROWS, HD), bf16),
            sized((ACCR, ROWS), f32),
            sized((1, ROWS), f32),
            sized((LATC, HD), f32),
        ],
        in_specs=[SMEM, SMEM, SMEM] + [VMEM] * 8,
        out_specs=[ANY, VMEM, VMEM, VMEM],
        scratch_shapes=[
            pltpu.VMEM((ROWS, HD), f32),
            pltpu.VMEM((ROWS, HD), f32),
            pltpu.VMEM((ROWS, ROWS), f32),
            pltpu.VMEM((2, 3, ROWS, HD), bf16),
            pltpu.SemaphoreType.DMA((2,)),
        ],
        cost_estimate=pl.CostEstimate(
            flops=heads * pair_ops, bytes_accessed=6 * ROWS * features * 2, transcendentals=0
        ),
        compiler_params=pltpu.CompilerParams(vmem_limit_bytes=ROOM),
        name="local",
    )(
        lengths, step_sizes, scal, place, select, turn, w_turned, modulation,
        q, k, v,
    )

    acc = table = None
    for c in range(count):
        final = c == count - 1
        here = [i for i in (c - 1, c) if i >= 0]
        operands = [scal, select, turn, w_turned, modulation, turned]
        specs = [SMEM, VMEM, VMEM, VMEM, VMEM, ANY]
        operands += [from_left[i] for i in here] + [from_right[i] for i in here]
        specs += [ANY] * (2 * len(here))
        if c > 0:
            operands += [table, acc]
            specs += [VMEM, VMEM]
        acc_shape = sized((2, ACCR, ROWS), f32)
        if final:
            operands.append(local_acc)
            specs.append(VMEM)
            out_shape = [
                sized((ACCR, ROWS), f32),
                sized((ACCR, REACH), f32),
                sized((ACCR, REACH), f32),
            ]
        elif c == 0:
            out_shape = [acc_shape, sized((2, 2, REACH, HD), f32)]
        else:
            out_shape = [acc_shape]
        scratch = [
            pltpu.VMEM((2, 3, SPAN, HD), bf16),
            pltpu.VMEM((2, 3, 2 * FAR + sum(chunks[i] for i in here), TILE, HD), bf16),
            pltpu.VMEM((2, ROWS, HD), f32),
            pltpu.SemaphoreType.DMA((2,)),
            pltpu.SemaphoreType.DMA((2, 3)),
        ]
        if final:
            scratch.append(pltpu.VMEM((2, ACCR, ROWS), f32))
        results = pl.pallas_call(
            functools.partial(cut_kernel, heads, chunks, c),
            out_shape=out_shape,
            in_specs=specs,
            out_specs=[VMEM] * len(out_shape),
            scratch_shapes=scratch,
            cost_estimate=pl.CostEstimate(
                flops=heads * pair_ops // count, bytes_accessed=4 << 20, transcendentals=0
            ),
            compiler_params=pltpu.CompilerParams(vmem_limit_bytes=ROOM),
        )(*operands)
        if final:
            own, back_left, back_right = results
        elif c == 0:
            acc, table = results
        else:
            (acc,) = results

    guided = pl.pallas_call(
        functools.partial(finish_kernel, features, ring),
        out_shape=sized((LATC // 2, ROWS), f32),
        in_specs=[VMEM, VMEM, VMEM, VMEM, SMEM],
        out_specs=VMEM,
        scratch_shapes=[
            pltpu.VMEM((ACCR, REACH), f32),
            pltpu.VMEM((ACCR, REACH), f32),
            pltpu.VMEM((LATC, ROWS), f32),
            pltpu.VMEM((LATC // 2, ROWS), f32),
            pltpu.SemaphoreType.DMA((3,)),
            pltpu.SemaphoreType.DMA((3,)),
        ],
        compiler_params=pltpu.CompilerParams(
            collective_id=0, has_side_effects=True, vmem_limit_bytes=ROOM
        ),
        name="finish",
    )(own, back_left, back_right, shift, guide_scale)
    return (latents.T + steps * guided).T


def solution(mesh):
    in_specs = (
        P("cfg", "req", None),
        P("cfg", "req", None),
        P("cfg", "req", None),
        P(None, "req"),
        P("req", "cfg"),
        P(),
        P(),
        P(),
        P(),
        P(),
    )
    return jax.shard_map(
        per_device, mesh=mesh, in_specs=in_specs, out_specs=P("req", "cfg"), check_vma=False
    )
```
